512 devices in a mesh: ctx: 64 (over z, x, core), head: 8 (over y).
Axes of the slice: x: 4, y: 8, z: 8, core: 2. Of those that a mesh axis runs over, the one named last changes fastest.
Arguments:
- queries: bfloat16 [8192, 36864], P('ctx', 'head'), may hold values from -6 to 6
- latents: bfloat16 [16384, 576], P('ctx'), may hold values from -5 to 5
- up_value: bfloat16 [512, 8192], P(None, 'head'), may hold values from -0.25 to 0.25
- grad_out: bfloat16 [8192, 8192], P('ctx', 'head'), may hold values from -12 to 12
- out_saved: bfloat16 [8192, 8192], P('ctx', 'head'), may hold values from -6 to 6
- log_sums: float32 [8192, 64], P('ctx', 'head'), as said below
- doc_starts: int32 [257], replicated, may hold values from 0 to 16384, as said below
Outputs:
- grad_queries: bfloat16 [8192, 36864], P('ctx', 'head')
- grad_latents: float32 [16384, 576], P(('ctx', 'head'))
- grad_up_value: float32 [512, 8192], P('ctx', 'head')
The draws below stay inside these ranges and needn't reach their ends.
Inputs may be any that keep to these rules, and one draw needn't show every extreme that they name: doc_starts[0] is 0; the entries rise strictly until they reach 16384 and then stay at 16384; consecutive entries differ by at most 512, and some document has exactly 512 positions. log_sums[t, h] is the log of the sum of exp(score[t, h, s]) over the keys s allowed for query t, computed from these queries and latents.
All inputs are finite; a program needn't handle non-finite values.
Results may differ from the reference program's by a relative error of at most 0.0085.
Values may be sent and summed in bfloat16 or wider, within the bound.
A program may use at most 64 MiB of HBM per device.

```python
import jax
import jax.numpy as jnp
from jax import lax

LAT = 512
ROPE = 64
FEAT = 576
VDIM = 128
HEADS = 64
Q_DEV = 128
KEY_DEV = 256
SPAN = 2
DOC_MAX = 512
KEYS = 16384
QUERIES = 8192
DOCS = 257


softmax_scale = 192.0 ** (-0.5)


def doc_index_drawn(positions, doc_starts):
    return jnp.sum((doc_starts[None, :] <= positions[:, None]).astype(jnp.int32), axis=1) - 1


def draw_world(key):
    key = jax.random.fold_in(key, 7)
    key_gap, key_pick, key_lat, key_query, key_lscale, key_qscale = jax.random.split(key, 6)
    gaps = jax.random.randint(key_gap, (DOCS - 1,), DOC_MAX // 8, DOC_MAX + 1)
    pick = jax.random.randint(key_pick, (), 0, 2)
    gaps = jnp.where(jnp.arange(DOCS - 1) == pick, DOC_MAX, gaps)
    starts = jnp.concatenate([jnp.zeros((1,), jnp.int32), jnp.cumsum(gaps).astype(jnp.int32)])
    starts = jnp.minimum(starts, KEYS).astype(jnp.int32)
    latents = jnp.clip(jax.random.normal(key_lat, (KEYS, FEAT), jnp.float32), -5.0, 5.0)
    queries = jnp.clip(jax.random.normal(key_query, (QUERIES, HEADS, FEAT), jnp.float32), -5.0, 5.0)
    latents = latents.astype(jnp.bfloat16)
    queries = queries.astype(jnp.bfloat16)
    padded = jnp.concatenate([jnp.zeros((SPAN * KEY_DEV, FEAT), jnp.bfloat16), latents], axis=0)
    window = (SPAN + 1) * KEY_DEV

    def one_block(block_id):
        query_block = lax.dynamic_slice_in_dim(queries, block_id * Q_DEV, Q_DEV, 0).astype(jnp.float32)
        key_block = lax.dynamic_slice_in_dim(padded, block_id * KEY_DEV, window, 0).astype(jnp.float32)
        query_pos = (block_id * KEY_DEV + KEY_DEV - Q_DEV + jnp.arange(Q_DEV)).astype(jnp.int32)
        key_pos = (block_id * KEY_DEV - SPAN * KEY_DEV + jnp.arange(window)).astype(jnp.int32)
        allowed = (doc_index_drawn(query_pos, starts)[:, None] == doc_index_drawn(key_pos, starts)[None, :]) & (key_pos[None, :] <= query_pos[:, None])
        scores = jnp.einsum('thf,sf->ths', query_block, key_block) * softmax_scale
        scores = jnp.where(allowed[:, None, :], scores, -jnp.inf)
        top = jnp.max(scores, axis=2, keepdims=True)
        return top[:, :, 0] + jnp.log(jnp.sum(jnp.exp(scores - top), axis=2))
    sums = lax.map(one_block, jnp.arange(KEYS // KEY_DEV).astype(jnp.int32)).reshape(QUERIES, HEADS)
    return (starts, latents, queries.reshape(QUERIES, HEADS * FEAT), sums)


def draw_doc_starts(key, part):
    return draw_world(key)[0]


def draw_latents(key, part):
    return draw_world(key)[1]


def draw_queries(key, part):
    return draw_world(key)[2]


def draw_log_sums(key, part):
    return draw_world(key)[3].astype(jnp.float32)


def shard_levels(key, dims, shards, smallest, high):
    loudness, own = 1.0, jax.random.fold_in(key, 6)
    for position, shards_of in shards:
        steps = jnp.exp(jax.random.uniform(jax.random.fold_in(own, position), (shards_of,), jnp.float32, smallest / len(shards), high / len(shards)))
        loudness = loudness * jnp.repeat(steps, dims[position] // shards_of).reshape([-1 if axis == position else 1 for axis in range(len(dims))])
    return loudness


def bell_draw(own_key, shape, spread, bound, cuts=(), kind=jnp.bfloat16):
    entries = spread * jax.random.normal(own_key, shape, jnp.float32)
    if cuts:
        entries = entries * shard_levels(own_key, shape, cuts, -0.22, 0.18)
    return jnp.clip(entries, -bound, bound).astype(kind)


def setup_inputs(seed: int = 0) -> dict:
    streams_of = jax.random.split(jax.random.key(seed), 8)
    queries = draw_queries(jax.random.fold_in(streams_of[7], 71), 0)
    latents = draw_latents(jax.random.fold_in(streams_of[7], 71), 0)
    up_value = bell_draw(streams_of[2], (LAT, HEADS * VDIM), LAT ** -0.5, 0.25, ((1, 8),))
    grad_out = bell_draw(streams_of[3], (QUERIES, HEADS * VDIM), 2.0, 12.0, ((0, 64), (1, 8)))
    out_saved = bell_draw(streams_of[4], (QUERIES, HEADS * VDIM), 1.0, 6.0, ((0, 64), (1, 8)))
    log_sums = draw_log_sums(jax.random.fold_in(streams_of[7], 71), 0)
    doc_starts = draw_doc_starts(jax.random.fold_in(streams_of[7], 71), 0)
    return {"queries": queries, "latents": latents, "up_value": up_value, "grad_out": grad_out, "out_saved": out_saved, "log_sums": log_sums, "doc_starts": doc_starts}


softmax_scale = 192.0 ** -0.5


def doc_index(positions, doc_starts):
    return jnp.sum((doc_starts[None, :] <= positions[:, None]).astype(jnp.int32), axis=1) - 1


def reference(queries, latents, up_value, grad_out, out_saved, log_sums, doc_starts):
    query_heads = queries.reshape(QUERIES, HEADS, FEAT)
    grad_heads = grad_out.reshape(QUERIES, HEADS, VDIM)
    saved_heads = out_saved.reshape(QUERIES, HEADS, VDIM)
    weight_heads = up_value.reshape(LAT, HEADS, VDIM).astype(jnp.float32)
    padded = jnp.concatenate([jnp.zeros((SPAN * KEY_DEV, FEAT), latents.dtype), latents], axis=0)
    window = (SPAN + 1) * KEY_DEV
    block_count = KEYS // KEY_DEV

    def step(carry, block_id):
        grad_lat_pad, grad_weight = carry
        query_block = lax.dynamic_slice_in_dim(query_heads, block_id * Q_DEV, Q_DEV, 0).astype(jnp.float32)
        grad_block = lax.dynamic_slice_in_dim(grad_heads, block_id * Q_DEV, Q_DEV, 0).astype(jnp.float32)
        saved_block = lax.dynamic_slice_in_dim(saved_heads, block_id * Q_DEV, Q_DEV, 0).astype(jnp.float32)
        sums_block = lax.dynamic_slice_in_dim(log_sums, block_id * Q_DEV, Q_DEV, 0)
        key_block = lax.dynamic_slice_in_dim(padded, block_id * KEY_DEV, window, 0).astype(jnp.float32)
        query_pos = (block_id * KEY_DEV + KEY_DEV - Q_DEV + jnp.arange(Q_DEV)).astype(jnp.int32)
        key_pos = (block_id * KEY_DEV - SPAN * KEY_DEV + jnp.arange(window)).astype(jnp.int32)
        allowed = (doc_index(query_pos, doc_starts)[:, None] == doc_index(key_pos, doc_starts)[None, :]) & (key_pos[None, :] <= query_pos[:, None])
        grad_lat_q = jnp.einsum("thv,jhv->thj", grad_block, weight_heads).astype(jnp.bfloat16).astype(jnp.float32)
        row_delta = jnp.sum(grad_block * saved_block, axis=2)
        scores = jnp.einsum("thf,sf->ths", query_block, key_block) * softmax_scale
        prob_full = jnp.where(allowed[:, None, :], jnp.exp(scores - sums_block[:, :, None]), 0.0)
        prob_half = prob_full.astype(jnp.bfloat16).astype(jnp.float32)
        values = key_block[:, :LAT]
        out_lat = jnp.einsum("ths,sj->thj", prob_half, values).astype(jnp.bfloat16).astype(jnp.float32)
        grad_prob = jnp.einsum("thj,sj->ths", grad_lat_q, values)
        grad_score = (prob_full * (grad_prob - row_delta[:, :, None]) * softmax_scale).astype(jnp.bfloat16).astype(jnp.float32)
        grad_query = jnp.einsum("ths,sf->thf", grad_score, key_block).astype(jnp.bfloat16)
        grad_key = jnp.einsum("ths,thf->sf", grad_score, query_block)
        grad_value = jnp.einsum("ths,thj->sj", prob_half, grad_lat_q)
        grad_key = grad_key + jnp.pad(grad_value, ((0, 0), (0, ROPE)))
        start = (block_id * KEY_DEV).astype(jnp.int32)
        current = lax.dynamic_slice_in_dim(grad_lat_pad, start, window, 0)
        grad_lat_pad = lax.dynamic_update_slice_in_dim(grad_lat_pad, current + grad_key, start, 0)
        grad_weight = grad_weight + jnp.einsum("thj,thv->jhv", out_lat, grad_block)
        return (grad_lat_pad, grad_weight), grad_query.reshape(Q_DEV, HEADS * FEAT)

    start_carry = (jnp.zeros((SPAN * KEY_DEV + KEYS, FEAT), jnp.float32), jnp.zeros((LAT, HEADS, VDIM), jnp.float32))
    (grad_lat_pad, grad_weight), grad_blocks = lax.scan(step, start_carry, jnp.arange(block_count).astype(jnp.int32))
    grad_queries = grad_blocks.reshape(QUERIES, HEADS * FEAT)
    grad_latents = grad_lat_pad[SPAN * KEY_DEV:]
    return grad_queries, grad_latents, grad_weight.reshape(LAT, HEADS * VDIM)
```

```python
import functools

import jax
import jax.numpy as jnp
from jax import lax
from jax.experimental import pallas as pl
from jax.experimental.pallas import tpu as pltpu
from jax.sharding import PartitionSpec as P

SCALE = 192.0 ** (-0.5)
MESH = pl.DeviceIdType.MESH
NX, NZ, NC, NY = 4, 8, 2, 8
CTX = NX * NZ * NC
F32, BF16 = jnp.float32, jnp.bfloat16


def dot(a, b, ca, cb):
    return lax.dot_general(a, b, (((ca,), (cb,)), ((), ())), preferred_element_type=F32)


def barrier(peers):
    sem = pltpu.get_barrier_semaphore()
    for peer in peers:
        pl.semaphore_signal(sem, inc=1, device_id=peer, device_id_type=MESH)
    pl.semaphore_wait(sem, len(peers))


def shift_kernel(own_ref, prev_ref, send_sem, recv_sem):
    d, y = lax.axis_index("ctx"), lax.axis_index("head")
    at = lambda step: (lax.rem(d + step + CTX, CTX), y)
    barrier([at(1), at(-1), at(2), at(-2)])
    near = pltpu.make_async_remote_copy(
        own_ref, prev_ref.at[pl.ds(128, 256)], send_sem.at[0], recv_sem.at[0], at(1), MESH
    )
    far = pltpu.make_async_remote_copy(
        own_ref.at[pl.ds(128, 128)], prev_ref.at[pl.ds(0, 128)], send_sem.at[1], recv_sem.at[1],
        at(2), MESH,
    )
    near.start()
    far.start()
    near.wait()
    far.wait()


def shift(latents):
    return pl.pallas_call(
        shift_kernel,
        out_shape=jax.ShapeDtypeStruct((384, 576), BF16),
        in_specs=[pl.BlockSpec(memory_space=pltpu.VMEM)],
        out_specs=pl.BlockSpec(memory_space=pltpu.VMEM),
        scratch_shapes=[pltpu.SemaphoreType.DMA((2,)), pltpu.SemaphoreType.DMA((2,))],
        compiler_params=pltpu.CompilerParams(collective_id=0, has_side_effects=True),
        name="shift",
    )(latents)


def compute_kernel(
    q_ref, own_ref, prev_ref, w_ref, g_ref, o_ref, ls_ref, ds_ref,
    gq_ref, gkp_ref, gko_ref, t_ref,
    ck, qs, gl, pb, gs, gqs, ol, gk,
):
    d = lax.axis_index("ctx")
    ck[0, pl.ds(0, 384), pl.ds(0, 576)] = prev_ref[...]
    ck[0, pl.ds(384, 256), pl.ds(0, 576)] = own_ref[...]
    ck[0, :, pl.ds(576, 64)] = jnp.zeros((640, 64), BF16)
    ck[1] = pltpu.roll(ck[0].astype(F32), 64, 1).astype(BF16)

    qpos = d * 256 + 128 + lax.broadcasted_iota(jnp.int32, (128, 1), 0)
    starts = ds_ref[...]
    begin = jnp.max(jnp.where(starts <= qpos, starts, 0), axis=1, keepdims=True)
    kpos = d * 256 - 384 + lax.broadcasted_iota(jnp.int32, (128, 640), 1)
    allowed = (kpos >= begin) & (kpos <= qpos)

    for par in range(2):
        for i in range(4):
            rows = pl.ds(i * 128, 128)
            h = 2 * i + par
            qs[par, rows, :] = q_ref[:, pl.ds(i * 1152 + par * 512, 640)]
            gl[par, rows, :] = dot(
                g_ref[:, pl.ds(h * 128, 128)], w_ref[:, pl.ds(h * 128, 128)], 1, 1
            ).astype(BF16)

    for par in range(2):
        score = dot(qs[par], ck[par], 1, 1)
        gprob = dot(gl[par], ck[0, :, pl.ds(0, 512)], 1, 1)
        for i in range(4):
            rows = pl.ds(i * 128, 128)
            h = 2 * i + par
            cols = pl.ds(h * 128, 128)
            delta = jnp.sum(
                g_ref[:, cols].astype(F32) * o_ref[:, cols].astype(F32), axis=1, keepdims=True
            )
            part = slice(i * 128, (i + 1) * 128)
            prob = jnp.where(allowed, jnp.exp(score[part] * SCALE - ls_ref[:, pl.ds(h, 1)]), 0.0)
            pb[par, rows, :] = prob.astype(BF16)
            gs[par, rows, :] = (prob * (gprob[part] - delta) * SCALE).astype(BF16)
        ol[par] = dot(pb[par], ck[0, :, pl.ds(0, 512)], 1, 0).astype(BF16)
        gqs[par] = dot(gs[par], ck[par], 1, 0)
        gk[par] = dot(gs[par], qs[par], 0, 0)
        gk[0, :, pl.ds(0, 512)] += dot(pb[par], gl[par], 0, 0)
        for i in range(4):
            h = 2 * i + par
            term = dot(
                ol[par, pl.ds(i * 128, 128), :], g_ref[:, pl.ds(h * 128, 128)], 0, 0
            ).astype(BF16)
            term = term.reshape(NZ, NX, 16, 128)
            for x in range(NX):
                t_ref[h // 4, x, :, :, pl.ds((h % 4) * 128, 128)] = term[:, x]

    for i in range(4):
        rows = pl.ds(i * 128, 128)
        even, odd = gqs[0, rows, :], gqs[1, rows, :]
        gq_ref[:, pl.ds(i * 1152, 512)] = even[:, :512].astype(BF16)
        gq_ref[:, pl.ds(i * 1152 + 512, 128)] = (even[:, 512:] + odd[:, :128]).astype(BF16)
        gq_ref[:, pl.ds(i * 1152 + 640, 512)] = odd[:, 128:].astype(BF16)
    total = gk[0] + pltpu.roll(gk[1], 576, 1)
    gkp_ref[...] = total[:384, :576].astype(BF16)
    gko_ref[...] = total[384:, :576]


def compute(queries, own, prev, up_value, grad_out, out_saved, log_sums, doc_starts):
    vmem = pl.BlockSpec(memory_space=pltpu.VMEM)
    return pl.pallas_call(
        compute_kernel,
        out_shape=(
            jax.ShapeDtypeStruct((128, 4608), BF16),
            jax.ShapeDtypeStruct((384, 576), BF16),
            jax.ShapeDtypeStruct((256, 576), F32),
            jax.ShapeDtypeStruct((2, NX, NZ, 16, 512), BF16),
        ),
        in_specs=[vmem] * 8,
        out_specs=(vmem,) * 4,
        scratch_shapes=[
            pltpu.VMEM((2, 640, 640), BF16),
            pltpu.VMEM((2, 512, 640), BF16),
            pltpu.VMEM((2, 512, 512), BF16),
            pltpu.VMEM((2, 512, 640), BF16),
            pltpu.VMEM((2, 512, 640), BF16),
            pltpu.VMEM((2, 512, 640), F32),
            pltpu.VMEM((2, 512, 512), BF16),
            pltpu.VMEM((2, 640, 640), F32),
        ],
        compiler_params=pltpu.CompilerParams(vmem_limit_bytes=56 << 20),
        name="attend",
    )(queries, own, prev, up_value, grad_out, out_saved, log_sums, doc_starts)


def reduce_kernel(
    gkp_ref, gko_ref, t_ref, gl_ref, gw_ref,
    back_near, back_far, ysend, yrecv, crecv, xsend, xrecv, zsend, zrecv, fin, frecv,
    s_back, r_back, s_y, r_y, s_c, r_c, s_x, r_x, s_z, r_z, s_f, r_f,
):
    d, y = lax.axis_index("ctx"), lax.axis_index("head")
    z, x, c = d // 8, lax.rem(d // 2, 4), lax.rem(d, 2)
    ring = lambda step: (lax.rem(d + step + CTX, CTX), y)
    partner = (d + 1 - 2 * c, y)
    at_x = lambda step: (z * 8 + lax.rem(x + step, 4) * 2 + c, y)
    at_z = lambda step: (lax.rem(z + step, 8) * 8 + x * 2 + c, y)
    at_y = lambda step: (d, lax.rem(y + step, 8))
    barrier(
        [ring(1), ring(-1), ring(2), ring(-2), partner]
        + [at_x(k) for k in range(1, NX)]
        + [at_z(k) for k in range(1, NZ)]
        + [at_y(k) for k in range(1, NY)]
    )

    def remote(src, dst, send, recv, to):
        copy = pltpu.make_async_remote_copy(src, dst, send, recv, to, MESH)
        copy.start()
        return copy

    near = remote(gkp_ref.at[pl.ds(128, 256)], back_near, s_back.at[0], r_back.at[0], ring(-1))
    far = remote(gkp_ref.at[pl.ds(0, 128)], back_far, s_back.at[1], r_back.at[1], ring(-2))
    cores = []
    for k in range(1, NX + 1):
        xi = lax.rem(x + k, 4)
        cores.append(
            remote(t_ref.at[1 - c, xi], crecv.at[xi], s_c.at[k - 1], r_c.at[k - 1], partner)
        )

    xs = []
    for k in range(1, NX):
        xi = lax.rem(x + k, 4)
        cores[k - 1].wait_recv()
        xsend[k - 1] = (t_ref[c, xi].astype(F32) + crecv[xi].astype(F32)).astype(BF16)
        xs.append(remote(xsend.at[k - 1], xrecv.at[k - 1], s_x.at[k - 1], r_x.at[k - 1], at_x(k)))

    near.wait_recv()
    far.wait_recv()
    total = gko_ref[...] + back_near[...].astype(F32)
    total = jnp.concatenate([total[:128], total[128:] + back_far[...].astype(F32)], axis=0)
    ysend[...] = total.astype(BF16).reshape(NY, 32, 576)
    ys = []
    for k in range(1, NY):
        ys.append(
            remote(
                ysend.at[lax.rem(y + k, 8)], yrecv.at[k - 1], s_y.at[k - 1], r_y.at[k - 1], at_y(k)
            )
        )

    cores[NX - 1].wait_recv()
    part = t_ref[c, x].astype(F32) + crecv[x].astype(F32)
    for k in range(1, NX):
        xs[k - 1].wait_recv()
        part = part + xrecv[k - 1].astype(F32)
    zsend[...] = part.astype(BF16)
    zs = []
    for k in range(1, NZ):
        zs.append(
            remote(
                zsend.at[lax.rem(z + k, 8)], zrecv.at[k - 1], s_z.at[k - 1], r_z.at[k - 1], at_z(k)
            )
        )

    mine = ysend[y].astype(F32)
    for k in range(1, NY):
        ys[k - 1].wait_recv()
        mine = mine + yrecv[k - 1].astype(F32)
    gl_ref[...] = mine

    last = zsend[z].astype(F32)
    for k in range(1, NZ):
        zs[k - 1].wait_recv()
        last = last + zrecv[k - 1].astype(F32)
    fin[...] = last.reshape(2, 8, 512)
    swap = remote(fin.at[1 - c], frecv, s_f, r_f, partner)
    gw_ref[:, pl.ds(pl.multiple_of(c * 512, 512), 512)] = fin[c]
    swap.wait_recv()
    gw_ref[:, pl.ds(pl.multiple_of((1 - c) * 512, 512), 512)] = frecv[...]
    for copy in [near, far, swap] + cores + xs + ys + zs:
        copy.wait_send()


def reduce(gk_prev, gk_own, terms):
    vmem = pl.BlockSpec(memory_space=pltpu.VMEM)
    dma = pltpu.SemaphoreType.DMA
    return pl.pallas_call(
        reduce_kernel,
        out_shape=(
            jax.ShapeDtypeStruct((32, 576), F32),
            jax.ShapeDtypeStruct((8, 1024), F32),
        ),
        in_specs=[vmem] * 3,
        out_specs=(vmem,) * 2,
        scratch_shapes=[
            pltpu.VMEM((256, 576), BF16),
            pltpu.VMEM((128, 576), BF16),
            pltpu.VMEM((NY, 32, 576), BF16),
            pltpu.VMEM((NY - 1, 32, 576), BF16),
            pltpu.VMEM((NX, NZ, 16, 512), BF16),
            pltpu.VMEM((NX - 1, NZ, 16, 512), BF16),
            pltpu.VMEM((NX - 1, NZ, 16, 512), BF16),
            pltpu.VMEM((NZ, 16, 512), BF16),
            pltpu.VMEM((NZ - 1, 16, 512), BF16),
            pltpu.VMEM((2, 8, 512), F32),
            pltpu.VMEM((8, 512), F32),
            dma((2,)), dma((2,)),
            dma((NY - 1,)), dma((NY - 1,)),
            dma((NX,)), dma((NX,)),
            dma((NX - 1,)), dma((NX - 1,)),
            dma((NZ - 1,)), dma((NZ - 1,)),
            dma, dma,
        ],
        compiler_params=pltpu.CompilerParams(
            collective_id=1, has_side_effects=True, vmem_limit_bytes=32 << 20
        ),
        name="reduce",
    )(gk_prev, gk_own, terms)


def on_device(queries, latents, up_value, grad_out, out_saved, log_sums, doc_starts):
    prev = shift(latents)
    grad_queries, gk_prev, gk_own, terms = compute(
        queries, latents, prev, up_value, grad_out, out_saved, log_sums, doc_starts.reshape(1, -1)
    )
    grad_latents, grad_up_value = reduce(gk_prev, gk_own, terms)
    return (grad_queries, grad_latents, grad_up_value)


def solution(mesh):
    return jax.shard_map(
        on_device,
        mesh=mesh,
        in_specs=(
            P("ctx", "head"),
            P("ctx", None),
            P(None, "head"),
            P("ctx", "head"),
            P("ctx", "head"),
            P("ctx", "head"),
            P(),
        ),
        out_specs=(P("ctx", "head"), P(("ctx", "head"), None), P("ctx", "head")),
        check_vma=False,
    )
```

```python
import jax
import jax.numpy as jnp
from jax import lax
from jax.experimental import pallas as pl
from jax.experimental.pallas import tpu as pltpu
from jax.sharding import PartitionSpec as P

SCALE = 192.0 ** (-0.5)
MESH = pl.DeviceIdType.MESH
NX, NZ, NC, NY = 4, 8, 2, 8
CTX = NX * NZ * NC
F32, BF16 = jnp.float32, jnp.bfloat16
OWN, NEAR, FAR = (0, 256), (256, 256), (512, 128)


def dot(a, b, ca, cb):
    return lax.dot_general(a, b, (((ca,), (cb,)), ((), ())), preferred_element_type=F32)


def kernel(
    q_hbm, ct_hbm, w_hbm, g_hbm, o_hbm, ls_hbm, ds_ref,
    gq_hbm, gl_ref, gw_ref,
    qv, wv, gv, ov, lsv, win, qs, gl, pb, gs, ol, gqv, delta, lsc,
    gko, nbuf, nrecv, ya, yarecv, yb, ybrecv, ybsum, bsend, brecv,
    tv, crecv, xsend, xrecv, zpart, zsend, zrecv, fin, frecv,
    s_in, s_out, s_sh, r_sh, s_n, r_n, s_ya, r_ya, s_yb, r_yb, s_b, r_b,
    s_c, r_c, s_x, r_x, s_z, r_z, s_f, r_f,
):
    d, y = lax.axis_index("ctx"), lax.axis_index("head")
    z, x, c = d // 8, lax.rem(d // 2, 4), lax.rem(d, 2)
    ring = lambda step: (lax.rem(d + step + CTX, CTX), y)
    partner = (d + 1 - 2 * c, y)
    at_x = lambda step: (z * 8 + lax.rem(x + step, 4) * 2 + c, y)
    at_z = lambda step: (lax.rem(z + step, 8) * 8 + x * 2 + c, y)
    at_y = lambda step: (d, lax.rem(y + step, 8))

    def remote(src, dst, send, recv, to):
        return pltpu.make_async_remote_copy(src, dst, send, recv, to, MESH)

    feats = pl.ds(64, 576)
    loads = [
        pltpu.make_async_copy(ct_hbm, win.at[feats, pl.ds(0, 256)], s_in.at[0]),
        pltpu.make_async_copy(g_hbm, gv, s_in.at[1]),
        pltpu.make_async_copy(w_hbm, wv, s_in.at[2]),
        pltpu.make_async_copy(q_hbm, qv, s_in.at[3]),
        pltpu.make_async_copy(ls_hbm, lsv, s_in.at[4]),
        pltpu.make_async_copy(o_hbm, ov, s_in.at[5]),
    ]
    for load in loads:
        load.start()

    peers = (
        [ring(1), ring(-1), ring(2), ring(-2), partner]
        + [at_x(k) for k in range(1, NX)]
        + [at_y(k) for k in range(1, NY)]
        + [at_z(k) for k in range(1, NZ)]
    )
    entry = pltpu.get_barrier_semaphore()
    for peer in peers:
        pl.semaphore_signal(entry, inc=1, device_id=peer, device_id_type=MESH)
    win[pl.ds(0, 64), :] = jnp.zeros((64, 640), BF16)
    win[pl.ds(640, 64), :] = jnp.zeros((64, 640), BF16)
    loads[0].wait()
    pl.semaphore_wait(entry, len(peers))
    near = remote(
        win.at[feats, pl.ds(0, 256)], win.at[feats, pl.ds(256, 256)], s_sh.at[0], r_sh.at[0],
        ring(1),
    )
    far = remote(
        win.at[feats, pl.ds(128, 128)], win.at[feats, pl.ds(512, 128)], s_sh.at[1], r_sh.at[1],
        ring(2),
    )
    near.start()
    far.start()

    for load in loads[1:]:
        load.wait()
    lsc[...] = lsv[...].T
    for par in range(2):
        for i in range(4):
            rows = pl.ds(i * 128, 128)
            h = 2 * i + par
            cols = pl.ds(h * 128, 128)
            qs[par, rows, :] = qv[:, pl.ds(i * 1152 + par * 512, 640)]
            gl[par, rows, :] = dot(gv[:, cols], wv[:, cols], 1, 1).astype(BF16)
            delta[:, pl.ds(h, 1)] = jnp.sum(
                gv[:, cols].astype(F32) * ov[:, cols].astype(F32), axis=1, keepdims=True
            )
    qpos = d * 256 + 128 + lax.broadcasted_iota(jnp.int32, (128, 1), 0)
    starts = ds_ref[...]
    begin = jnp.max(jnp.where(starts <= qpos, starts, 0), axis=1, keepdims=True)

    def attend(par, block, base):
        first, count = block
        lanes = pl.ds(first, count)
        score = dot(qs[par], win[pl.ds(64 - 64 * par, 640), lanes], 1, 0)
        gprob = dot(gl[par], win[pl.ds(64, 512), lanes], 1, 0)
        kpos = base + lax.broadcasted_iota(jnp.int32, (128, count), 1)
        allowed = (kpos >= begin) & (kpos <= qpos)
        for i in range(4):
            rows = pl.ds(i * 128, 128)
            part = slice(i * 128, (i + 1) * 128)
            h = pl.ds(2 * i + par, 1)
            prob = jnp.where(allowed, jnp.exp(score[part] * SCALE - lsc[:, h]), 0.0)
            pb[par, rows, lanes] = prob.astype(BF16)
            gs[par, rows, lanes] = (prob * (gprob[part] - delta[:, h]) * SCALE).astype(BF16)
        part = dot(pb[par, :, lanes], win[pl.ds(64, 512), lanes], 1, 1)
        return part

    def key_grad(block):
        lanes = pl.ds(*block)
        even = dot(gs[0, :, lanes], qs[0], 0, 0)
        odd = pltpu.roll(dot(gs[1, :, lanes], qs[1], 0, 0), 576, 1)
        value = dot(pb[0, :, lanes], gl[0], 0, 0) + dot(pb[1, :, lanes], gl[1], 0, 0)
        both = even + odd
        return jnp.concatenate([both[:, :512] + value, both[:, 512:576]], axis=1)

    for par in range(2):
        ol[par] = attend(par, OWN, d * 256)
    gko[...] = key_grad(OWN)

    near.wait_recv()
    for par in range(2):
        ol[par] += attend(par, NEAR, d * 256 - 256)
    far.wait_recv()

    cores, xs, zs, swaps = [[], []], [[], []], [[], []], []

    def up_grad(par):
        lat = (ol[par] + attend(par, FAR, d * 256 - 384)).astype(BF16)
        for i in range(4):
            h = 2 * i + par
            term = dot(lat[i * 128 : (i + 1) * 128], gv[:, pl.ds(h * 128, 128)], 0, 0)
            term = term.astype(BF16).reshape(NZ, NX, 16, 128)
            for xi in range(NX):
                tv[par, i // 2, xi, :, :, pl.ds((i % 2) * 128, 128)] = term[:, xi]
        for k in range(1, NX + 1):
            xi = lax.rem(x + k, 4)
            j = par * NX + k - 1
            copy = remote(
                tv.at[par, 1 - c, xi], crecv.at[par, xi], s_c.at[j], r_c.at[j], partner
            )
            copy.start()
            cores[par].append(copy)

    def stage_x(par):
        for k in range(1, NX):
            xi = lax.rem(x + k, 4)
            j = par * (NX - 1) + k - 1
            cores[par][k - 1].wait_recv()
            xsend[j] = (tv[par, c, xi].astype(F32) + crecv[par, xi].astype(F32)).astype(BF16)
            copy = remote(xsend.at[j], xrecv.at[j], s_x.at[j], r_x.at[j], at_x(k))
            copy.start()
            xs[par].append(copy)
        cores[par][NX - 1].wait_recv()
        zpart[par] = tv[par, c, x].astype(F32) + crecv[par, x].astype(F32)

    def stage_z(par):
        part = zpart[par]
        for k in range(1, NX):
            xs[par][k - 1].wait_recv()
            part = part + xrecv[par * (NX - 1) + k - 1].astype(F32)
        zsend[par] = part.astype(BF16)
        for k in range(1, NZ):
            j = par * (NZ - 1) + k - 1
            copy = remote(
                zsend.at[par, lax.rem(z + k, 8)], zrecv.at[j], s_z.at[j], r_z.at[j], at_z(k)
            )
            copy.start()
            zs[par].append(copy)

    def stage_swap(par):
        last = zsend[par, z].astype(F32)
        for k in range(1, NZ):
            zs[par][k - 1].wait_recv()
            last = last + zrecv[par * (NZ - 1) + k - 1].astype(F32)
        fin[par] = last.reshape(2, 8, 256)
        copy = remote(fin.at[par, 1 - c], frecv.at[par], s_f.at[par], r_f.at[par], partner)
        copy.start()
        swaps.append(copy)

    up_grad(0)
    up_grad(1)
    stage_x(0)

    near_grad = key_grad(NEAR)
    nbuf[...] = near_grad.astype(BF16)
    whole = remote(nbuf, nrecv, s_n, r_n, partner)
    half = remote(
        nbuf.at[pl.ds(128, 128)], nrecv.at[pl.ds(0, 128)], s_n, r_n, partner
    )

    @pl.when(c == 1)
    def _():
        whole.start()

    @pl.when(c == 0)
    def _():
        half.start()

    stage_x(1)
    gkf = key_grad(FAR)
    yb[pl.ds(0, 4)] = near_grad[:128].reshape(4, 32, 576).astype(BF16)

    @pl.when(c == 0)
    def _():
        whole.wait_recv()
        gko[...] += nrecv[...].astype(F32)
        yb[pl.ds(4, 4)] = gkf.reshape(4, 32, 576).astype(BF16)

    @pl.when(c == 1)
    def _():
        half.wait_recv()
        yb[pl.ds(4, 4)] = (
            (gkf + nrecv[pl.ds(0, 128)].astype(F32)).reshape(4, 32, 576).astype(BF16)
        )

    ybs, yas = [], []
    for k in range(1, NY):
        to = lax.rem(y + k, 8)
        copy = remote(yb.at[to], ybrecv.at[k - 1], s_yb.at[k - 1], r_yb.at[k - 1], at_y(k))
        ybs.append(copy)

        @pl.when((c == 0) | (to >= 4))
        def _():
            copy.start()

    ya[...] = gko[...].reshape(NY, 32, 576).astype(BF16)
    for k in range(1, NY):
        to = lax.rem(y + k, 8)
        copy = remote(ya.at[to], yarecv.at[k - 1], s_ya.at[k - 1], r_ya.at[k - 1], at_y(k))
        copy.start()
        yas.append(copy)

    def query_grad(par):
        return dot(gs[par], win[pl.ds(64 - 64 * par, 640), :], 1, 1)

    even = query_grad(0)
    stage_z(0)
    odd = query_grad(1)
    for i in range(4):
        rows = slice(i * 128, (i + 1) * 128)
        gqv[:, pl.ds(i * 1152, 512)] = even[rows, :512].astype(BF16)
        gqv[:, pl.ds(i * 1152 + 512, 128)] = (even[rows, 512:] + odd[rows, :128]).astype(BF16)
        gqv[:, pl.ds(i * 1152 + 640, 512)] = odd[rows, 128:].astype(BF16)
    store = pltpu.make_async_copy(gqv, gq_hbm, s_out)
    store.start()
    stage_z(1)

    back = remote(
        bsend, brecv, s_b, r_b, ring(jnp.where((c == 1) | (y >= 4), -2, -1))
    )

    @pl.when((c == 0) | (y >= 4))
    def _():
        mine = yb[y].astype(F32)
        for k in range(1, NY):
            ybs[k - 1].wait_recv()
            mine = mine + ybrecv[k - 1].astype(F32)
        bsend[...] = mine.astype(BF16)
        back.start()

    stage_swap(0)
    mine = ya[y].astype(F32)
    for k in range(1, NY):
        yas[k - 1].wait_recv()
        mine = mine + yarecv[k - 1].astype(F32)
    gl_ref[...] = mine

    @pl.when((c == 1) | (y >= 4))
    def _():
        back.wait_recv()
        gl_ref[...] += brecv[...].astype(F32)

    stage_swap(1)
    for par in range(2):
        for side in range(2):
            half_of = c if side == 0 else 1 - c
            if side == 1:
                swaps[par].wait_recv()
            value = fin[par, c] if side == 0 else frecv[par]
            for i in range(2):
                col = half_of * 512 + i * 256 + par * 128
                gw_ref[:, pl.ds(pl.multiple_of(col, 128), 128)] = value[:, i * 128 : i * 128 + 128]

    near.wait_send()
    far.wait_send()

    @pl.when(c == 1)
    def _():
        whole.wait_send()

    @pl.when(c == 0)
    def _():
        half.wait_send()

    for k in range(1, NY):
        @pl.when((c == 0) | (lax.rem(y + k, 8) >= 4))
        def _():
            ybs[k - 1].wait_send()

    @pl.when((c == 0) | (y >= 4))
    def _():
        back.wait_send()

    for copy in yas + cores[0] + cores[1] + xs[0] + xs[1] + zs[0] + zs[1] + swaps:
        copy.wait_send()
    store.wait()


def on_device(queries, latents, up_value, grad_out, out_saved, log_sums, doc_starts):
    anywhere = pl.BlockSpec(memory_space=pl.ANY)
    vmem = pl.BlockSpec(memory_space=pltpu.VMEM)
    dma = pltpu.SemaphoreType.DMA
    shapes = [
        ((128, 4608), BF16), ((512, 1024), BF16), ((128, 1024), BF16), ((128, 1024), BF16),
        ((8, 128), F32), ((704, 640), BF16), ((2, 512, 640), BF16), ((2, 512, 512), BF16),
        ((2, 512, 640), BF16), ((2, 512, 640), BF16), ((2, 512, 512), F32), ((128, 4608), BF16),
        ((128, 8), F32), ((128, 8), F32),
        ((256, 576), F32), ((256, 576), BF16), ((256, 576), BF16),
        ((NY, 32, 576), BF16), ((NY - 1, 32, 576), BF16),
        ((NY, 32, 576), BF16), ((NY - 1, 32, 576), BF16),
        ((32, 576), F32), ((32, 576), BF16), ((32, 576), BF16),
        ((2, 2, NX, NZ, 16, 256), BF16), ((2, NX, NZ, 16, 256), BF16),
        ((2 * (NX - 1), NZ, 16, 256), BF16), ((2 * (NX - 1), NZ, 16, 256), BF16),
        ((2, NZ, 16, 256), F32), ((2, NZ, 16, 256), BF16), ((2 * (NZ - 1), 16, 256), BF16),
        ((2, 2, 8, 256), F32), ((2, 8, 256), F32),
    ]
    return pl.pallas_call(
        kernel,
        out_shape=(
            jax.ShapeDtypeStruct((128, 4608), BF16),
            jax.ShapeDtypeStruct((32, 576), F32),
            jax.ShapeDtypeStruct((8, 1024), F32),
        ),
        in_specs=[anywhere] * 6 + [vmem],
        out_specs=(anywhere, vmem, vmem),
        scratch_shapes=[pltpu.VMEM(shape, kind) for shape, kind in shapes]
        + [
            dma((6,)), dma, dma((2,)), dma((2,)), dma, dma,
            dma((NY - 1,)), dma((NY - 1,)), dma((NY - 1,)), dma((NY - 1,)), dma, dma,
            dma((2 * NX,)), dma((2 * NX,)), dma((2 * NX - 2,)), dma((2 * NX - 2,)),
            dma((2 * NZ - 2,)), dma((2 * NZ - 2,)), dma((2,)), dma((2,)),
        ],
        compiler_params=pltpu.CompilerParams(
            collective_id=0, has_side_effects=True, vmem_limit_bytes=58 << 20
        ),
        name="latent_attention_backward",
    )(queries, latents.T, up_value, grad_out, out_saved, log_sums.T, doc_starts.reshape(1, -1))


def solution(mesh):
    return jax.shard_map(
        on_device,
        mesh=mesh,
        in_specs=(
            P("ctx", "head"),
            P("ctx", None),
            P(None, "head"),
            P("ctx", "head"),
            P("ctx", "head"),
            P("ctx", "head"),
            P(),
        ),
        out_specs=(P("ctx", "head"), P(("ctx", "head"), None), P("ctx", "head")),
        check_vma=False,
    )
```

```python
import jax
import jax.numpy as jnp
from jax import lax
from jax.experimental import pallas as pl
from jax.experimental.pallas import tpu as pltpu
from jax.sharding import PartitionSpec as P

SCALE = 192.0 ** (-0.5)
MESH = pl.DeviceIdType.MESH
NX, NZ, NC, NY = 4, 8, 2, 8
CTX = NX * NZ * NC
F32, BF16 = jnp.float32, jnp.bfloat16
OWN, NEAR, FAR = (0, 256), (256, 256), (512, 128)


def dot(a, b, ca, cb):
    return lax.dot_general(a, b, (((ca,), (cb,)), ((), ())), preferred_element_type=F32)


def kernel(
    q_hbm, ct_hbm, w_hbm, g_hbm, o_hbm, ls_hbm, ds_ref,
    gq_hbm, gl_ref, gw_ref,
    qv, wv, gv, ov, lsv, win, qs, gl, pb, gs, ol, gqv, delta, lsc,
    gko, nbuf, nrecv, ya, yarecv, yb, ybrecv, ybsum, bsend, brecv,
    tv, crecv, xsend, xrecv, zpart, zsend, zrecv, fin, frecv,
    s_in, s_out, s_sh, r_sh, s_n, r_n, s_ya, r_ya, s_yb, r_yb, s_b, r_b,
    s_c, r_c, s_x, r_x, s_z, r_z, s_f, r_f,
):
    d, y = lax.axis_index("ctx"), lax.axis_index("head")
    z, x, c = d // 8, lax.rem(d // 2, 4), lax.rem(d, 2)
    ring = lambda step: (lax.rem(d + step + CTX, CTX), y)
    partner = (d + 1 - 2 * c, y)
    at_x = lambda step: (z * 8 + lax.rem(x + step, 4) * 2 + c, y)
    at_z = lambda step: (lax.rem(z + step, 8) * 8 + x * 2 + c, y)
    at_y = lambda step: (d, lax.rem(y + step, 8))

    def remote(src, dst, send, recv, to):
        return pltpu.make_async_remote_copy(src, dst, send, recv, to, MESH)

    feats = pl.ds(64, 576)
    loads = [
        pltpu.make_async_copy(ct_hbm, win.at[feats, pl.ds(0, 256)], s_in.at[0]),
        pltpu.make_async_copy(g_hbm, gv, s_in.at[1]),
        pltpu.make_async_copy(w_hbm, wv, s_in.at[2]),
        pltpu.make_async_copy(q_hbm, qv, s_in.at[3]),
        pltpu.make_async_copy(ls_hbm, lsv, s_in.at[4]),
        pltpu.make_async_copy(o_hbm, ov, s_in.at[5]),
    ]
    for load in loads:
        load.start()

    peers = (
        [ring(1), ring(-1), ring(2), ring(-2), partner]
        + [at_x(k) for k in range(1, NX)]
        + [at_y(k) for k in range(1, NY)]
        + [at_z(k) for k in range(1, NZ)]
    )
    entry = pltpu.get_barrier_semaphore()
    for peer in peers:
        pl.semaphore_signal(entry, inc=1, device_id=peer, device_id_type=MESH)
    win[pl.ds(0, 64), :] = jnp.zeros((64, 640), BF16)
    win[pl.ds(640, 64), :] = jnp.zeros((64, 640), BF16)
    loads[0].wait()
    pl.semaphore_wait(entry, len(peers))
    near = remote(
        win.at[feats, pl.ds(0, 256)], win.at[feats, pl.ds(256, 256)], s_sh.at[0], r_sh.at[0],
        ring(1),
    )
    far = remote(
        win.at[feats, pl.ds(128, 128)], win.at[feats, pl.ds(512, 128)], s_sh.at[1], r_sh.at[1],
        ring(2),
    )
    near.start()
    far.start()

    for load in loads[1:]:
        load.wait()
    lsc[...] = lsv[...].T
    for par in range(2):
        for i in range(4):
            rows = pl.ds(i * 128, 128)
            h = 2 * i + par
            cols = pl.ds(h * 128, 128)
            qs[par, rows, :] = qv[:, pl.ds(i * 1152 + par * 512, 640)]
            gl[par, rows, :] = dot(gv[:, cols], wv[:, cols], 1, 1).astype(BF16)
            delta[:, pl.ds(h, 1)] = jnp.sum(
                gv[:, cols].astype(F32) * ov[:, cols].astype(F32), axis=1, keepdims=True
            )
    qpos = d * 256 + 128 + lax.broadcasted_iota(jnp.int32, (128, 1), 0)
    starts = ds_ref[...].reshape(1, 257)
    begin = jnp.max(jnp.where(starts <= qpos, starts, 0), axis=1, keepdims=True)

    def attend(par, block, base):
        first, count = block
        lanes = pl.ds(first, count)
        score = dot(qs[par], win[pl.ds(64 - 64 * par, 640), lanes], 1, 0)
        gprob = dot(gl[par], win[pl.ds(64, 512), lanes], 1, 0)
        kpos = base + lax.broadcasted_iota(jnp.int32, (128, count), 1)
        allowed = (kpos >= begin) & (kpos <= qpos)
        for i in range(4):
            rows = pl.ds(i * 128, 128)
            part = slice(i * 128, (i + 1) * 128)
            h = pl.ds(2 * i + par, 1)
            prob = jnp.where(allowed, jnp.exp(score[part] * SCALE - lsc[:, h]), 0.0)
            pb[par, rows, lanes] = prob.astype(BF16)
            gs[par, rows, lanes] = (prob * (gprob[part] - delta[:, h]) * SCALE).astype(BF16)
        part = dot(pb[par, :, lanes], win[pl.ds(64, 512), lanes], 1, 1)
        return part

    def key_grad(block):
        lanes = pl.ds(*block)
        even = dot(gs[0, :, lanes], qs[0], 0, 0)
        odd = pltpu.roll(dot(gs[1, :, lanes], qs[1], 0, 0), 576, 1)
        value = dot(pb[0, :, lanes], gl[0], 0, 0) + dot(pb[1, :, lanes], gl[1], 0, 0)
        both = even + odd
        return jnp.concatenate([both[:, :512] + value, both[:, 512:576]], axis=1)

    for par in range(2):
        ol[par] = attend(par, OWN, d * 256)
    gko[...] = key_grad(OWN)

    whole = remote(nbuf, nrecv, s_n, r_n, partner)
    half = remote(
        nbuf.at[pl.ds(128, 128)], nrecv.at[pl.ds(0, 128)], s_n, r_n, partner
    )

    def attend_near():
        near.wait_recv()
        for par in range(2):
            ol[par] += attend(par, NEAR, d * 256 - 256)

    @pl.when(c == 1)
    def _():
        attend_near()
        nbuf[...] = key_grad(NEAR).astype(BF16)
        whole.start()

    @pl.when(c == 0)
    def _():
        whole.wait_recv()
        gko[...] += nrecv[...].astype(F32)

    ya[...] = gko[...].reshape(NY, 32, 576).astype(BF16)
    ybs, yas = [], []
    for k in range(1, NY):
        to = lax.rem(y + k, 8)
        copy = remote(ya.at[to], yarecv.at[k - 1], s_ya.at[k - 1], r_ya.at[k - 1], at_y(k))
        copy.start()
        yas.append(copy)

    @pl.when(c == 0)
    def _():
        attend_near()

    far.wait_recv()

    cores, xs, zs, swaps = [[], []], [[], []], [[], []], []

    def up_grad(par):
        lat = (ol[par] + attend(par, FAR, d * 256 - 384)).astype(BF16)
        for i in range(4):
            h = 2 * i + par
            term = dot(lat[i * 128 : (i + 1) * 128], gv[:, pl.ds(h * 128, 128)], 0, 0)
            term = term.astype(BF16).reshape(NZ, NX, 16, 128)
            for xi in range(NX):
                tv[par, i // 2, xi, :, :, pl.ds((i % 2) * 128, 128)] = term[:, xi]
        for k in range(1, NX + 1):
            xi = lax.rem(x + k, 4)
            j = par * NX + k - 1
            copy = remote(
                tv.at[par, 1 - c, xi], crecv.at[par, xi], s_c.at[j], r_c.at[j], partner
            )
            copy.start()
            cores[par].append(copy)

    def stage_x(par):
        for k in range(1, NX):
            xi = lax.rem(x + k, 4)
            j = par * (NX - 1) + k - 1
            cores[par][k - 1].wait_recv()
            xsend[j] = (tv[par, c, xi].astype(F32) + crecv[par, xi].astype(F32)).astype(BF16)
            copy = remote(xsend.at[j], xrecv.at[j], s_x.at[j], r_x.at[j], at_x(k))
            copy.start()
            xs[par].append(copy)
        cores[par][NX - 1].wait_recv()
        zpart[par] = tv[par, c, x].astype(F32) + crecv[par, x].astype(F32)

    def stage_z(par):
        part = zpart[par]
        for k in range(1, NX):
            xs[par][k - 1].wait_recv()
            part = part + xrecv[par * (NX - 1) + k - 1].astype(F32)
        zsend[par] = part.astype(BF16)
        for k in range(1, NZ):
            j = par * (NZ - 1) + k - 1
            copy = remote(
                zsend.at[par, lax.rem(z + k, 8)], zrecv.at[j], s_z.at[j], r_z.at[j], at_z(k)
            )
            copy.start()
            zs[par].append(copy)

    def stage_swap(par):
        last = zsend[par, z].astype(F32)
        for k in range(1, NZ):
            zs[par][k - 1].wait_recv()
            last = last + zrecv[par * (NZ - 1) + k - 1].astype(F32)
        fin[par] = last.reshape(2, 8, 256)
        copy = remote(fin.at[par, 1 - c], frecv.at[par], s_f.at[par], r_f.at[par], partner)
        copy.start()
        swaps.append(copy)

    up_grad(0)
    up_grad(1)
    stage_x(0)

    @pl.when(c == 0)
    def _():
        near_grad = key_grad(NEAR)
        nbuf[...] = near_grad.astype(BF16)
        half.start()
        yb[pl.ds(0, 4)] = near_grad[:128].reshape(4, 32, 576).astype(BF16)

    stage_x(1)
    gkf = key_grad(FAR)

    @pl.when(c == 0)
    def _():
        yb[pl.ds(4, 4)] = gkf.reshape(4, 32, 576).astype(BF16)

    @pl.when(c == 1)
    def _():
        half.wait_recv()
        yb[pl.ds(4, 4)] = (
            (gkf + nrecv[pl.ds(0, 128)].astype(F32)).reshape(4, 32, 576).astype(BF16)
        )

    for k in range(1, NY):
        to = lax.rem(y + k, 8)
        copy = remote(yb.at[to], ybrecv.at[k - 1], s_yb.at[k - 1], r_yb.at[k - 1], at_y(k))
        ybs.append(copy)

        @pl.when((c == 0) | (to >= 4))
        def _():
            copy.start()

    def query_grad(par):
        return dot(gs[par], win[pl.ds(64 - 64 * par, 640), :], 1, 1)

    even = query_grad(0)
    stage_z(0)
    odd = query_grad(1)
    for i in range(4):
        rows = slice(i * 128, (i + 1) * 128)
        gqv[:, pl.ds(i * 1152, 512)] = even[rows, :512].astype(BF16)
        gqv[:, pl.ds(i * 1152 + 512, 128)] = (even[rows, 512:] + odd[rows, :128]).astype(BF16)
        gqv[:, pl.ds(i * 1152 + 640, 512)] = odd[rows, 128:].astype(BF16)
    store = pltpu.make_async_copy(gqv, gq_hbm, s_out)
    store.start()
    stage_z(1)

    back = remote(
        bsend, brecv, s_b, r_b, ring(jnp.where((c == 1) | (y >= 4), -2, -1))
    )

    @pl.when((c == 0) | (y >= 4))
    def _():
        mine = yb[y].astype(F32)
        for k in range(1, NY):
            ybs[k - 1].wait_recv()
            mine = mine + ybrecv[k - 1].astype(F32)
        bsend[...] = mine.astype(BF16)
        back.start()

    stage_swap(0)
    mine = ya[y].astype(F32)
    for k in range(1, NY):
        yas[k - 1].wait_recv()
        mine = mine + yarecv[k - 1].astype(F32)
    gl_ref[...] = mine

    @pl.when((c == 1) | (y >= 4))
    def _():
        back.wait_recv()
        gl_ref[...] += brecv[...].astype(F32)

    stage_swap(1)
    for par in range(2):
        for side in range(2):
            half_of = c if side == 0 else 1 - c
            if side == 1:
                swaps[par].wait_recv()
            value = fin[par, c] if side == 0 else frecv[par]
            for i in range(2):
                col = half_of * 512 + i * 256 + par * 128
                gw_ref[:, pl.ds(pl.multiple_of(col, 128), 128)] = value[:, i * 128 : i * 128 + 128]

    near.wait_send()
    far.wait_send()

    @pl.when(c == 1)
    def _():
        whole.wait_send()

    @pl.when(c == 0)
    def _():
        half.wait_send()

    for k in range(1, NY):
        @pl.when((c == 0) | (lax.rem(y + k, 8) >= 4))
        def _():
            ybs[k - 1].wait_send()

    @pl.when((c == 0) | (y >= 4))
    def _():
        back.wait_send()

    for copy in yas + cores[0] + cores[1] + xs[0] + xs[1] + zs[0] + zs[1] + swaps:
        copy.wait_send()
    store.wait()


def settle_kernel(gq_in, gl_in, gw_in, gq_out, gl_out, gw_out, gqv, glv, gwv, s_in, s_out):
    parts = [(gl_in, glv, gl_out), (gw_in, gwv, gw_out)]
    for i in range(8):
        rows = pl.ds(16 * i, 16)
        parts.append((gq_in.at[rows], gqv.at[rows], gq_out.at[rows]))
    reads = [pltpu.make_async_copy(a, v, s_in.at[i]) for i, (a, v, _) in enumerate(parts)]
    writes = [pltpu.make_async_copy(v, b, s_out.at[i]) for i, (_, v, b) in enumerate(parts)]
    for read in reads:
        read.start()
    for read, write in zip(reads, writes):
        read.wait()
        write.start()
    for write in writes:
        write.wait()


def on_device(queries, latents, up_value, grad_out, out_saved, log_sums, doc_starts):
    anywhere = pl.BlockSpec(memory_space=pl.ANY)
    vmem = pl.BlockSpec(memory_space=pltpu.VMEM)
    dma = pltpu.SemaphoreType.DMA
    shapes = [
        ((128, 4608), BF16), ((512, 1024), BF16), ((128, 1024), BF16), ((128, 1024), BF16),
        ((8, 128), F32), ((704, 640), BF16), ((2, 512, 640), BF16), ((2, 512, 512), BF16),
        ((2, 512, 640), BF16), ((2, 512, 640), BF16), ((2, 512, 512), F32), ((128, 4608), BF16),
        ((128, 8), F32), ((128, 8), F32),
        ((256, 576), F32), ((256, 576), BF16), ((256, 576), BF16),
        ((NY, 32, 576), BF16), ((NY - 1, 32, 576), BF16),
        ((NY, 32, 576), BF16), ((NY - 1, 32, 576), BF16),
        ((32, 576), F32), ((32, 576), BF16), ((32, 576), BF16),
        ((2, 2, NX, NZ, 16, 256), BF16), ((2, NX, NZ, 16, 256), BF16),
        ((2 * (NX - 1), NZ, 16, 256), BF16), ((2 * (NX - 1), NZ, 16, 256), BF16),
        ((2, NZ, 16, 256), F32), ((2, NZ, 16, 256), BF16), ((2 * (NZ - 1), 16, 256), BF16),
        ((2, 2, 8, 256), F32), ((2, 8, 256), F32),
    ]
    results = pl.pallas_call(
        kernel,
        out_shape=(
            jax.ShapeDtypeStruct((128, 4608), BF16),
            jax.ShapeDtypeStruct((32, 576), F32),
            jax.ShapeDtypeStruct((8, 1024), F32),
        ),
        in_specs=[anywhere] * 6 + [vmem],
        out_specs=(anywhere, vmem, vmem),
        scratch_shapes=[pltpu.VMEM(shape, kind) for shape, kind in shapes]
        + [
            dma((6,)), dma, dma((2,)), dma((2,)), dma, dma,
            dma((NY - 1,)), dma((NY - 1,)), dma((NY - 1,)), dma((NY - 1,)), dma, dma,
            dma((2 * NX,)), dma((2 * NX,)), dma((2 * NX - 2,)), dma((2 * NX - 2,)),
            dma((2 * NZ - 2,)), dma((2 * NZ - 2,)), dma((2,)), dma((2,)),
        ],
        compiler_params=pltpu.CompilerParams(
            collective_id=0, has_side_effects=True, vmem_limit_bytes=58 << 20
        ),
        name="latent_attention_backward",
    )(queries, latents.T, up_value, grad_out, out_saved, log_sums.T, doc_starts)
    return pl.pallas_call(
        settle_kernel,
        out_shape=tuple(jax.ShapeDtypeStruct(r.shape, r.dtype) for r in results),
        in_specs=[anywhere] * 3,
        out_specs=(anywhere,) * 3,
        scratch_shapes=[pltpu.VMEM(r.shape, r.dtype) for r in results] + [dma((10,)), dma((10,))],
        name="settle",
    )(*results)


def solution(mesh):
    return jax.shard_map(
        on_device,
        mesh=mesh,
        in_specs=(
            P("ctx", "head"),
            P("ctx", None),
            P(None, "head"),
            P("ctx", "head"),
            P("ctx", "head"),
            P("ctx", "head"),
            P(),
        ),
        out_specs=(P("ctx", "head"), P(("ctx", "head"), None), P("ctx", "head")),
        check_vma=False,
    )
```

```python
import jax
import jax.numpy as jnp
from jax import lax
from jax.experimental import pallas as pl
from jax.experimental.pallas import tpu as pltpu
from jax.sharding import PartitionSpec as P

SCALE = 192.0 ** (-0.5)
MESH = pl.DeviceIdType.MESH
NX, NZ, NC, NY = 4, 8, 2, 8
CTX = NX * NZ * NC
F32, BF16 = jnp.float32, jnp.bfloat16
OWN, NEAR, FAR = (0, 256), (256, 256), (512, 128)


def dot(a, b, ca, cb):
    return lax.dot_general(a, b, (((ca,), (cb,)), ((), ())), preferred_element_type=F32)


def kernel(
    q_hbm, ct_hbm, w_hbm, g_hbm, o_hbm, ls_hbm, ds_ref,
    gq_hbm, gl_ref, gw_ref,
    qv, wv, gv, ov, lsv, win, qs, gl, pb, gs, ol, gqv, delta, lsc,
    gko, nbuf, nrecv, ya, yarecv, yb, ybrecv, ybsum, bsend, brecv,
    tv, crecv, xsend, xrecv, zpart, zsend, zrecv, fin, frecv,
    s_in, s_out, s_sh, r_sh, s_n, r_n, s_ya, r_ya, s_yb, r_yb, s_b, r_b,
    s_c, r_c, s_x, r_x, s_z, r_z, s_f, r_f, known,
):
    d, y = lax.axis_index("ctx"), lax.axis_index("head")
    z, x, c = d // 8, lax.rem(d // 2, 4), lax.rem(d, 2)
    ring = lambda step: (lax.rem(d + step + CTX, CTX), y)
    partner = (d + 1 - 2 * c, y)
    at_x = lambda step: (z * 8 + lax.rem(x + step, 4) * 2 + c, y)
    at_z = lambda step: (lax.rem(z + step, 8) * 8 + x * 2 + c, y)
    at_y = lambda step: (d, lax.rem(y + step, 8))

    def remote(src, dst, send, recv, to):
        return pltpu.make_async_remote_copy(src, dst, send, recv, to, MESH)

    feats = pl.ds(64, 576)
    loads = [
        pltpu.make_async_copy(ct_hbm, win.at[feats, pl.ds(0, 256)], s_in.at[0]),
        pltpu.make_async_copy(g_hbm, gv, s_in.at[1]),
        pltpu.make_async_copy(w_hbm, wv, s_in.at[2]),
        pltpu.make_async_copy(q_hbm, qv, s_in.at[3]),
        pltpu.make_async_copy(ls_hbm, lsv, s_in.at[4]),
        pltpu.make_async_copy(o_hbm, ov, s_in.at[5]),
    ]
    for load in loads:
        load.start()

    sides = [at_y(1), at_y(NY - 1), at_z(1), at_z(NZ - 1)]

    def tell(level):
        for side in sides:
            pl.semaphore_signal(known.at[level], inc=1, device_id=side, device_id_type=MESH)

    def hear(level):
        pl.semaphore_wait(known.at[level], len(sides))

    peers = (
        [ring(1), ring(-1), ring(2), ring(-2), partner]
        + [at_x(k) for k in range(1, NX)]
        + sides
    )
    entry = pltpu.get_barrier_semaphore()
    for peer in peers:
        pl.semaphore_signal(entry, inc=1, device_id=peer, device_id_type=MESH)
    win[pl.ds(0, 64), :] = jnp.zeros((64, 640), BF16)
    win[pl.ds(640, 64), :] = jnp.zeros((64, 640), BF16)
    loads[0].wait()
    pl.semaphore_wait(entry, len(peers))
    near = remote(
        win.at[feats, pl.ds(0, 256)], win.at[feats, pl.ds(256, 256)], s_sh.at[0], r_sh.at[0],
        ring(1),
    )
    far = remote(
        win.at[feats, pl.ds(128, 128)], win.at[feats, pl.ds(512, 128)], s_sh.at[1], r_sh.at[1],
        ring(2),
    )
    near.start()
    far.start()
    tell(0)

    for load in loads[1:]:
        load.wait()
    lsc[...] = lsv[...].T
    for par in range(2):
        for i in range(4):
            rows = pl.ds(i * 128, 128)
            h = 2 * i + par
            cols = pl.ds(h * 128, 128)
            qs[par, rows, :] = qv[:, pl.ds(i * 1152 + par * 512, 640)]
            gl[par, rows, :] = dot(gv[:, cols], wv[:, cols], 1, 1).astype(BF16)
            delta[:, pl.ds(h, 1)] = jnp.sum(
                gv[:, cols].astype(F32) * ov[:, cols].astype(F32), axis=1, keepdims=True
            )
    qpos = d * 256 + 128 + lax.broadcasted_iota(jnp.int32, (128, 1), 0)
    starts = ds_ref[...].reshape(1, 257)
    begin = jnp.max(jnp.where(starts <= qpos, starts, 0), axis=1, keepdims=True)

    def attend(par, block, base):
        first, count = block
        lanes = pl.ds(first, count)
        score = dot(qs[par], win[pl.ds(64 - 64 * par, 640), lanes], 1, 0)
        gprob = dot(gl[par], win[pl.ds(64, 512), lanes], 1, 0)
        kpos = base + lax.broadcasted_iota(jnp.int32, (128, count), 1)
        allowed = (kpos >= begin) & (kpos <= qpos)
        for i in range(4):
            rows = pl.ds(i * 128, 128)
            part = slice(i * 128, (i + 1) * 128)
            h = pl.ds(2 * i + par, 1)
            prob = jnp.where(allowed, jnp.exp(score[part] * SCALE - lsc[:, h]), 0.0)
            pb[par, rows, lanes] = prob.astype(BF16)
            gs[par, rows, lanes] = (prob * (gprob[part] - delta[:, h]) * SCALE).astype(BF16)
        part = dot(pb[par, :, lanes], win[pl.ds(64, 512), lanes], 1, 1)
        return part

    def key_grad(block):
        lanes = pl.ds(*block)
        even = dot(gs[0, :, lanes], qs[0], 0, 0)
        odd = pltpu.roll(dot(gs[1, :, lanes], qs[1], 0, 0), 576, 1)
        value = dot(pb[0, :, lanes], gl[0], 0, 0) + dot(pb[1, :, lanes], gl[1], 0, 0)
        both = even + odd
        return jnp.concatenate([both[:, :512] + value, both[:, 512:576]], axis=1)

    ol[0] = attend(0, OWN, d * 256)
    hear(0)
    tell(1)
    ol[1] = attend(1, OWN, d * 256)
    hear(1)
    tell(2)
    gko[...] = key_grad(OWN)
    hear(2)

    whole = remote(nbuf, nrecv, s_n, r_n, partner)
    half = remote(nbuf.at[pl.ds(128, 128)], nrecv.at[pl.ds(0, 128)], s_n, r_n, partner)
    yas = [
        remote(
            ya.at[lax.rem(y + k, 8)], yarecv.at[k - 1], s_ya.at[k - 1], r_ya.at[k - 1], at_y(k)
        )
        for k in range(1, NY)
    ]
    ybs = [
        remote(
            yb.at[lax.rem(y + k, 8)], ybrecv.at[k - 1], s_yb.at[k - 1], r_yb.at[k - 1], at_y(k)
        )
        for k in range(1, NY)
    ]

    def send_own():
        ya[...] = gko[...].reshape(NY, 32, 576).astype(BF16)
        for copy in yas:
            copy.start()

    def attend_near(par):
        ol[par] += attend(par, NEAR, d * 256 - 256)

    @pl.when(c == 1)
    def _():
        send_own()
        near.wait_recv()
        attend_near(0)
        attend_near(1)
        nbuf[...] = key_grad(NEAR).astype(BF16)
        whole.start()

    @pl.when(c == 0)
    def _():
        near.wait_recv()
        attend_near(0)

    far.wait_recv()

    cores, xs, zs, swaps = [[], []], [[], []], [[], []], []

    def up_grad(par):
        lat = (ol[par] + attend(par, FAR, d * 256 - 384)).astype(BF16)
        for i in range(4):
            h = 2 * i + par
            term = dot(lat[i * 128 : (i + 1) * 128], gv[:, pl.ds(h * 128, 128)], 0, 0)
            term = term.astype(BF16).reshape(NZ, NX, 16, 128)
            for xi in range(NX):
                tv[par, i // 2, xi, :, :, pl.ds((i % 2) * 128, 128)] = term[:, xi]
        for k in range(1, NX + 1):
            xi = lax.rem(x + k, 4)
            j = par * NX + k - 1
            copy = remote(
                tv.at[par, 1 - c, xi], crecv.at[par, xi], s_c.at[j], r_c.at[j], partner
            )
            copy.start()
            cores[par].append(copy)

    def stage_x(par):
        for k in range(1, NX):
            xi = lax.rem(x + k, 4)
            j = par * (NX - 1) + k - 1
            cores[par][k - 1].wait_recv()
            xsend[j] = (tv[par, c, xi].astype(F32) + crecv[par, xi].astype(F32)).astype(BF16)
            copy = remote(xsend.at[j], xrecv.at[j], s_x.at[j], r_x.at[j], at_x(k))
            copy.start()
            xs[par].append(copy)
        cores[par][NX - 1].wait_recv()
        zpart[par] = tv[par, c, x].astype(F32) + crecv[par, x].astype(F32)

    def stage_z(par):
        part = zpart[par]
        for k in range(1, NX):
            xs[par][k - 1].wait_recv()
            part = part + xrecv[par * (NX - 1) + k - 1].astype(F32)
        zsend[par] = part.astype(BF16)
        for k in range(1, NZ):
            j = par * (NZ - 1) + k - 1
            copy = remote(
                zsend.at[par, lax.rem(z + k, 8)], zrecv.at[j], s_z.at[j], r_z.at[j], at_z(k)
            )
            copy.start()
            zs[par].append(copy)

    def stage_swap(par):
        last = zsend[par, z].astype(F32)
        for k in range(1, NZ):
            zs[par][k - 1].wait_recv()
            last = last + zrecv[par * (NZ - 1) + k - 1].astype(F32)
        fin[par] = last.reshape(2, 8, 256)
        copy = remote(fin.at[par, 1 - c], frecv.at[par], s_f.at[par], r_f.at[par], partner)
        copy.start()
        swaps.append(copy)

    up_grad(0)

    @pl.when(c == 0)
    def _():
        attend_near(1)
        whole.wait_recv()
        gko[...] += nrecv[...].astype(F32)
        send_own()

    stage_x(0)
    up_grad(1)

    @pl.when(c == 0)
    def _():
        near_grad = key_grad(NEAR)
        nbuf[...] = near_grad.astype(BF16)
        half.start()
        yb[pl.ds(0, 4)] = near_grad[:128].reshape(4, 32, 576).astype(BF16)
        for k in range(1, NY):
            @pl.when(lax.rem(y + k, 8) < 4)
            def _():
                ybs[k - 1].start()

    gkf = key_grad(FAR)
    stage_x(1)

    @pl.when(c == 0)
    def _():
        yb[pl.ds(4, 4)] = gkf.reshape(4, 32, 576).astype(BF16)

    @pl.when(c == 1)
    def _():
        half.wait_recv()
        yb[pl.ds(4, 4)] = (
            (gkf + nrecv[pl.ds(0, 128)].astype(F32)).reshape(4, 32, 576).astype(BF16)
        )

    for k in range(1, NY):
        @pl.when(lax.rem(y + k, 8) >= 4)
        def _():
            ybs[k - 1].start()

    def query_grad(par):
        return dot(gs[par], win[pl.ds(64 - 64 * par, 640), :], 1, 1)

    even = query_grad(0)
    stage_z(0)
    odd = query_grad(1)
    for i in range(4):
        rows = slice(i * 128, (i + 1) * 128)
        gq_hbm[:, pl.ds(i * 1152, 512)] = even[rows, :512].astype(BF16)
        gq_hbm[:, pl.ds(i * 1152 + 512, 128)] = (even[rows, 512:] + odd[rows, :128]).astype(BF16)
        gq_hbm[:, pl.ds(i * 1152 + 640, 512)] = odd[rows, 128:].astype(BF16)
    stage_z(1)

    back = remote(
        bsend, brecv, s_b, r_b, ring(jnp.where((c == 1) | (y >= 4), -2, -1))
    )

    @pl.when((c == 0) | (y >= 4))
    def _():
        mine = yb[y].astype(F32)
        for k in range(1, NY):
            ybs[k - 1].wait_recv()
            mine = mine + ybrecv[k - 1].astype(F32)
        bsend[...] = mine.astype(BF16)
        back.start()

    stage_swap(0)
    mine = ya[y].astype(F32)
    for k in range(1, NY):
        yas[k - 1].wait_recv()
        mine = mine + yarecv[k - 1].astype(F32)
    gl_ref[...] = mine

    @pl.when((c == 1) | (y >= 4))
    def _():
        back.wait_recv()
        gl_ref[...] += brecv[...].astype(F32)

    stage_swap(1)
    for par in range(2):
        for side in range(2):
            half_of = c if side == 0 else 1 - c
            if side == 1:
                swaps[par].wait_recv()
            value = fin[par, c] if side == 0 else frecv[par]
            for i in range(2):
                col = half_of * 512 + i * 256 + par * 128
                gw_ref[:, pl.ds(pl.multiple_of(col, 128), 128)] = value[:, i * 128 : i * 128 + 128]

    near.wait_send()
    far.wait_send()

    @pl.when(c == 1)
    def _():
        whole.wait_send()

    @pl.when(c == 0)
    def _():
        half.wait_send()

    for k in range(1, NY):
        @pl.when((c == 0) | (lax.rem(y + k, 8) >= 4))
        def _():
            ybs[k - 1].wait_send()

    @pl.when((c == 0) | (y >= 4))
    def _():
        back.wait_send()

    for copy in yas + cores[0] + cores[1] + xs[0] + xs[1] + zs[0] + zs[1] + swaps:
        copy.wait_send()


def settle_kernel(gq_in, gl_in, gw_in, gq_out, gl_out, gw_out, sem):
    pairs = [(gq_in, gq_out), (gl_in, gl_out), (gw_in, gw_out)]
    writes = [pltpu.make_async_copy(a, b, sem.at[i]) for i, (a, b) in enumerate(pairs)]
    for write in writes:
        write.start()
    for write in writes:
        write.wait()


def on_device(queries, latents, up_value, grad_out, out_saved, log_sums, doc_starts):
    anywhere = pl.BlockSpec(memory_space=pl.ANY)
    vmem = pl.BlockSpec(memory_space=pltpu.VMEM)
    dma = pltpu.SemaphoreType.DMA
    shapes = [
        ((128, 4608), BF16), ((512, 1024), BF16), ((128, 1024), BF16), ((128, 1024), BF16),
        ((8, 128), F32), ((704, 640), BF16), ((2, 512, 640), BF16), ((2, 512, 512), BF16),
        ((2, 512, 640), BF16), ((2, 512, 640), BF16), ((2, 512, 512), F32), ((128, 4608), BF16),
        ((128, 8), F32), ((128, 8), F32),
        ((256, 576), F32), ((256, 576), BF16), ((256, 576), BF16),
        ((NY, 32, 576), BF16), ((NY - 1, 32, 576), BF16),
        ((NY, 32, 576), BF16), ((NY - 1, 32, 576), BF16),
        ((32, 576), F32), ((32, 576), BF16), ((32, 576), BF16),
        ((2, 2, NX, NZ, 16, 256), BF16), ((2, NX, NZ, 16, 256), BF16),
        ((2 * (NX - 1), NZ, 16, 256), BF16), ((2 * (NX - 1), NZ, 16, 256), BF16),
        ((2, NZ, 16, 256), F32), ((2, NZ, 16, 256), BF16), ((2 * (NZ - 1), 16, 256), BF16),
        ((2, 2, 8, 256), F32), ((2, 8, 256), F32),
    ]
    results = pl.pallas_call(
        kernel,
        out_shape=(
            pltpu.VMEM((128, 4608), BF16),
            pltpu.VMEM((32, 576), F32),
            pltpu.VMEM((8, 1024), F32),
        ),
        in_specs=[anywhere] * 6 + [vmem],
        out_specs=(vmem, vmem, vmem),
        scratch_shapes=[pltpu.VMEM(shape, kind) for shape, kind in shapes]
        + [
            dma((6,)), dma, dma((2,)), dma((2,)), dma, dma,
            dma((NY - 1,)), dma((NY - 1,)), dma((NY - 1,)), dma((NY - 1,)), dma, dma,
            dma((2 * NX,)), dma((2 * NX,)), dma((2 * NX - 2,)), dma((2 * NX - 2,)),
            dma((2 * NZ - 2,)), dma((2 * NZ - 2,)), dma((2,)), dma((2,)),
            pltpu.SemaphoreType.REGULAR((3,)),
        ],
        compiler_params=pltpu.CompilerParams(
            collective_id=0, has_side_effects=True, vmem_limit_bytes=58 << 20
        ),
        name="latent_attention_backward",
    )(queries, latents.T, up_value, grad_out, out_saved, log_sums.T, doc_starts)
    return pl.pallas_call(
        settle_kernel,
        out_shape=tuple(jax.ShapeDtypeStruct(r.shape, r.dtype) for r in results),
        in_specs=[vmem] * 3,
        out_specs=(anywhere,) * 3,
        scratch_shapes=[dma((3,))],
        name="settle",
    )(*[pltpu.with_memory_space_constraint(r, pltpu.VMEM) for r in results])


def solution(mesh):
    return jax.shard_map(
        on_device,
        mesh=mesh,
        in_specs=(
            P("ctx", "head"),
            P("ctx", None),
            P(None, "head"),
            P("ctx", "head"),
            P("ctx", "head"),
            P("ctx", "head"),
            P(),
        ),
        out_specs=(P("ctx", "head"), P(("ctx", "head"), None), P("ctx", "head")),
        check_vma=False,
    )
```

```python
import jax
import jax.numpy as jnp
from jax import lax
from jax.experimental import pallas as pl
from jax.experimental.pallas import tpu as pltpu
from jax.sharding import PartitionSpec as P

SCALE = 192.0 ** (-0.5)
MESH = pl.DeviceIdType.MESH
NX, NZ, NC, NY = 4, 8, 2, 8
CTX = NX * NZ * NC
F32, BF16 = jnp.float32, jnp.bfloat16
OWN, NEAR, FAR = (0, 256), (256, 256), (512, 128)


def dot(a, b, ca, cb):
    return lax.dot_general(a, b, (((ca,), (cb,)), ((), ())), preferred_element_type=F32)


def kernel(
    q_hbm, ct_hbm, w_hbm, g_hbm, o_hbm, ls_hbm, ds_ref,
    gq_hbm, gl_ref, gw_ref,
    qv, wv, gv, ov, lsv, win, qs, gl, pb, gs, ol, gqv, delta, lsc,
    gko, nbuf, nrecv, ya, yarecv, yb, ybrecv, ybsum, bsend, brecv,
    tv, crecv, xsend, xrecv, zpart, zsend, zrecv,
    s_in, s_out, s_sh, r_sh, s_n, r_n, s_ya, r_ya, s_yb, r_yb, s_b, r_b,
    s_c, r_c, s_x, r_x, s_z, r_z, known,
):
    d, y = lax.axis_index("ctx"), lax.axis_index("head")
    z, x, c = d // 8, lax.rem(d // 2, 4), lax.rem(d, 2)
    ring = lambda step: (lax.rem(d + step + CTX, CTX), y)
    partner = (d + 1 - 2 * c, y)
    at_x = lambda step: (z * 8 + lax.rem(x + step, 4) * 2 + c, y)
    at_z = lambda step: (lax.rem(z + step, 8) * 8 + x * 2 + c, y)
    at_y = lambda step: (d, lax.rem(y + step, 8))

    def remote(src, dst, send, recv, to):
        return pltpu.make_async_remote_copy(src, dst, send, recv, to, MESH)

    feats = pl.ds(64, 576)
    loads = [
        pltpu.make_async_copy(ct_hbm, win.at[feats, pl.ds(0, 256)], s_in.at[0]),
        pltpu.make_async_copy(g_hbm, gv, s_in.at[1]),
        pltpu.make_async_copy(w_hbm, wv, s_in.at[2]),
        pltpu.make_async_copy(q_hbm, qv, s_in.at[3]),
        pltpu.make_async_copy(ls_hbm, lsv, s_in.at[4]),
        pltpu.make_async_copy(o_hbm, ov, s_in.at[5]),
    ]
    for load in loads:
        load.start()

    sides = [at_y(1), at_y(NY - 1), at_z(1), at_z(NZ - 1)]

    def tell(level):
        for side in sides:
            pl.semaphore_signal(known.at[level], inc=1, device_id=side, device_id_type=MESH)

    def hear(level):
        pl.semaphore_wait(known.at[level], len(sides))

    peers = (
        [ring(1), ring(-1), ring(2), ring(-2), partner]
        + [at_x(k) for k in range(1, NX)]
        + sides
    )
    entry = pltpu.get_barrier_semaphore()
    for peer in peers:
        pl.semaphore_signal(entry, inc=1, device_id=peer, device_id_type=MESH)
    win[pl.ds(0, 64), :] = jnp.zeros((64, 640), BF16)
    win[pl.ds(640, 64), :] = jnp.zeros((64, 640), BF16)
    loads[0].wait()
    pl.semaphore_wait(entry, len(peers))
    near = remote(
        win.at[feats, pl.ds(0, 256)], win.at[feats, pl.ds(256, 256)], s_sh.at[0], r_sh.at[0],
        ring(1),
    )
    far = remote(
        win.at[feats, pl.ds(128, 128)], win.at[feats, pl.ds(512, 128)], s_sh.at[1], r_sh.at[1],
        ring(2),
    )
    near.start()
    far.start()
    tell(0)

    for load in loads[1:]:
        load.wait()
    lsc[...] = lsv[...].T
    for par in range(2):
        for i in range(4):
            rows = pl.ds(i * 128, 128)
            h = 2 * i + par
            cols = pl.ds(h * 128, 128)
            qs[par, rows, :] = qv[:, pl.ds(i * 1152 + par * 512, 640)]
            gl[par, rows, :] = dot(gv[:, cols], wv[:, cols], 1, 1).astype(BF16)
            delta[:, pl.ds(h, 1)] = jnp.sum(
                gv[:, cols].astype(F32) * ov[:, cols].astype(F32), axis=1, keepdims=True
            )
    qpos = d * 256 + 128 + lax.broadcasted_iota(jnp.int32, (128, 1), 0)
    starts = ds_ref[...].reshape(1, 257)
    begin = jnp.max(jnp.where(starts <= qpos, starts, 0), axis=1, keepdims=True)

    def attend(par, block, base):
        first, count = block
        lanes = pl.ds(first, count)
        score = dot(qs[par], win[pl.ds(64 - 64 * par, 640), lanes], 1, 0)
        gprob = dot(gl[par], win[pl.ds(64, 512), lanes], 1, 0)
        kpos = base + lax.broadcasted_iota(jnp.int32, (128, count), 1)
        allowed = (kpos >= begin) & (kpos <= qpos)
        for i in range(4):
            rows = pl.ds(i * 128, 128)
            part = slice(i * 128, (i + 1) * 128)
            h = pl.ds(2 * i + par, 1)
            prob = jnp.where(allowed, jnp.exp(score[part] * SCALE - lsc[:, h]), 0.0)
            pb[par, rows, lanes] = prob.astype(BF16)
            gs[par, rows, lanes] = (prob * (gprob[part] - delta[:, h]) * SCALE).astype(BF16)
        part = dot(pb[par, :, lanes], win[pl.ds(64, 512), lanes], 1, 1)
        return part

    def key_grad(block):
        lanes = pl.ds(*block)
        even = dot(gs[0, :, lanes], qs[0], 0, 0)
        odd = pltpu.roll(dot(gs[1, :, lanes], qs[1], 0, 0), 576, 1)
        value = dot(pb[0, :, lanes], gl[0], 0, 0) + dot(pb[1, :, lanes], gl[1], 0, 0)
        both = even + odd
        return jnp.concatenate([both[:, :512] + value, both[:, 512:576]], axis=1)

    ol[0] = attend(0, OWN, d * 256)
    hear(0)
    tell(1)
    ol[1] = attend(1, OWN, d * 256)
    hear(1)
    tell(2)
    gko[...] = key_grad(OWN)
    hear(2)

    whole = remote(nbuf, nrecv, s_n, r_n, partner)
    half = remote(nbuf.at[pl.ds(128, 128)], nrecv.at[pl.ds(0, 128)], s_n, r_n, partner)
    yas = [
        remote(
            ya.at[lax.rem(y + k, 8)], yarecv.at[k - 1], s_ya.at[k - 1], r_ya.at[k - 1], at_y(k)
        )
        for k in range(1, NY)
    ]
    ybs = [
        remote(
            yb.at[lax.rem(y + k, 8)], ybrecv.at[k - 1], s_yb.at[k - 1], r_yb.at[k - 1], at_y(k)
        )
        for k in range(1, NY)
    ]

    def send_own():
        ya[...] = gko[...].reshape(NY, 32, 576).astype(BF16)
        for copy in yas:
            copy.start()

    def attend_near(par):
        ol[par] += attend(par, NEAR, d * 256 - 256)

    @pl.when(c == 1)
    def _():
        send_own()
        near.wait_recv()
        attend_near(0)
        attend_near(1)
        nbuf[...] = key_grad(NEAR).astype(BF16)
        whole.start()

    @pl.when(c == 0)
    def _():
        near.wait_recv()
        attend_near(0)

    far.wait_recv()

    cores, xs, zs = [[], []], [[], []], [[], []]

    def up_grad(par):
        lat = (ol[par] + attend(par, FAR, d * 256 - 384)).astype(BF16)
        for i in range(2):
            low, high = [
                dot(
                    lat[j * 128 : (j + 1) * 128], gv[:, pl.ds((2 * j + par) * 128, 128)], 0, 0
                ).reshape(NZ * NX * NC, 8, 128)
                for j in (i, i + 2)
            ]
            term = jnp.concatenate([low, high], axis=1).astype(BF16)
            term = term.reshape(NZ, NX, NC, 16, 128)
            for xi in range(NX):
                for ci in range(NC):
                    tv[par, ci, xi, :, :, pl.ds(i * 128, 128)] = term[:, xi, ci]
        for k in range(1, NX + 1):
            xi = lax.rem(x + k, 4)
            j = par * NX + k - 1
            copy = remote(
                tv.at[par, 1 - c, xi], crecv.at[par, xi], s_c.at[j], r_c.at[j], partner
            )
            copy.start()
            cores[par].append(copy)

    def stage_x(par):
        for k in range(1, NX):
            xi = lax.rem(x + k, 4)
            j = par * (NX - 1) + k - 1
            cores[par][k - 1].wait_recv()
            xsend[j] = (tv[par, c, xi].astype(F32) + crecv[par, xi].astype(F32)).astype(BF16)
            copy = remote(xsend.at[j], xrecv.at[j], s_x.at[j], r_x.at[j], at_x(k))
            copy.start()
            xs[par].append(copy)
        cores[par][NX - 1].wait_recv()
        zpart[par] = tv[par, c, x].astype(F32) + crecv[par, x].astype(F32)

    def stage_z(par):
        part = zpart[par]
        for k in range(1, NX):
            xs[par][k - 1].wait_recv()
            part = part + xrecv[par * (NX - 1) + k - 1].astype(F32)
        zsend[par] = part.astype(BF16)
        for k in range(1, NZ):
            j = par * (NZ - 1) + k - 1
            copy = remote(
                zsend.at[par, lax.rem(z + k, 8)], zrecv.at[j], s_z.at[j], r_z.at[j], at_z(k)
            )
            copy.start()
            zs[par].append(copy)

    def finish(par):
        last = zsend[par, z].astype(F32)
        for k in range(1, NZ):
            zs[par][k - 1].wait_recv()
            last = last + zrecv[par * (NZ - 1) + k - 1].astype(F32)
        for side in range(2):
            for i in range(2):
                gw_ref[:, pl.ds((2 * i + par + 4 * side) * 128, 128)] = last[
                    side * 8 : side * 8 + 8, i * 128 : i * 128 + 128
                ]

    up_grad(0)

    @pl.when(c == 0)
    def _():
        attend_near(1)
        whole.wait_recv()
        gko[...] += nrecv[...].astype(F32)
        send_own()

    stage_x(0)
    up_grad(1)

    @pl.when(c == 0)
    def _():
        near_grad = key_grad(NEAR)
        nbuf[...] = near_grad.astype(BF16)
        half.start()
        yb[pl.ds(0, 4)] = near_grad[:128].reshape(4, 32, 576).astype(BF16)
        for k in range(1, NY):
            @pl.when(lax.rem(y + k, 8) < 4)
            def _():
                ybs[k - 1].start()

    gkf = key_grad(FAR)
    stage_x(1)

    @pl.when(c == 0)
    def _():
        yb[pl.ds(4, 4)] = gkf.reshape(4, 32, 576).astype(BF16)

    @pl.when(c == 1)
    def _():
        half.wait_recv()
        yb[pl.ds(4, 4)] = (
            (gkf + nrecv[pl.ds(0, 128)].astype(F32)).reshape(4, 32, 576).astype(BF16)
        )

    for k in range(1, NY):
        @pl.when(lax.rem(y + k, 8) >= 4)
        def _():
            ybs[k - 1].start()

    def query_grad(par):
        return dot(gs[par], win[pl.ds(64 - 64 * par, 640), :], 1, 1)

    even = query_grad(0)
    stage_z(0)
    odd = query_grad(1)
    for i in range(4):
        rows = slice(i * 128, (i + 1) * 128)
        gq_hbm[:, pl.ds(i * 1152, 512)] = even[rows, :512].astype(BF16)
        gq_hbm[:, pl.ds(i * 1152 + 512, 128)] = (even[rows, 512:] + odd[rows, :128]).astype(BF16)
        gq_hbm[:, pl.ds(i * 1152 + 640, 512)] = odd[rows, 128:].astype(BF16)
    stage_z(1)

    back = remote(
        bsend, brecv, s_b, r_b, ring(jnp.where((c == 1) | (y >= 4), -2, -1))
    )

    @pl.when((c == 0) | (y >= 4))
    def _():
        mine = yb[y].astype(F32)
        for k in range(1, NY):
            ybs[k - 1].wait_recv()
            mine = mine + ybrecv[k - 1].astype(F32)
        bsend[...] = mine.astype(BF16)
        back.start()

    finish(0)
    mine = ya[y].astype(F32)
    for k in range(1, NY):
        yas[k - 1].wait_recv()
        mine = mine + yarecv[k - 1].astype(F32)
    gl_ref[...] = mine

    @pl.when((c == 1) | (y >= 4))
    def _():
        back.wait_recv()
        gl_ref[...] += brecv[...].astype(F32)

    finish(1)
    near.wait_send()
    far.wait_send()

    @pl.when(c == 1)
    def _():
        whole.wait_send()

    @pl.when(c == 0)
    def _():
        half.wait_send()

    for k in range(1, NY):
        @pl.when((c == 0) | (lax.rem(y + k, 8) >= 4))
        def _():
            ybs[k - 1].wait_send()

    @pl.when((c == 0) | (y >= 4))
    def _():
        back.wait_send()

    for copy in yas + cores[0] + cores[1] + xs[0] + xs[1] + zs[0] + zs[1]:
        copy.wait_send()


def settle_kernel(gq_in, gl_in, gw_in, gq_out, gl_out, gw_out, sem):
    pairs = [(gq_in, gq_out), (gl_in, gl_out), (gw_in, gw_out)]
    writes = [pltpu.make_async_copy(a, b, sem.at[i]) for i, (a, b) in enumerate(pairs)]
    for write in writes:
        write.start()
    for write in writes:
        write.wait()


def on_device(queries, latents, up_value, grad_out, out_saved, log_sums, doc_starts):
    anywhere = pl.BlockSpec(memory_space=pl.ANY)
    vmem = pl.BlockSpec(memory_space=pltpu.VMEM)
    dma = pltpu.SemaphoreType.DMA
    shapes = [
        ((128, 4608), BF16), ((512, 1024), BF16), ((128, 1024), BF16), ((128, 1024), BF16),
        ((8, 128), F32), ((704, 640), BF16), ((2, 512, 640), BF16), ((2, 512, 512), BF16),
        ((2, 512, 640), BF16), ((2, 512, 640), BF16), ((2, 512, 512), F32), ((128, 4608), BF16),
        ((128, 8), F32), ((128, 8), F32),
        ((256, 576), F32), ((256, 576), BF16), ((256, 576), BF16),
        ((NY, 32, 576), BF16), ((NY - 1, 32, 576), BF16),
        ((NY, 32, 576), BF16), ((NY - 1, 32, 576), BF16),
        ((32, 576), F32), ((32, 576), BF16), ((32, 576), BF16),
        ((2, 2, NX, NZ, 16, 256), BF16), ((2, NX, NZ, 16, 256), BF16),
        ((2 * (NX - 1), NZ, 16, 256), BF16), ((2 * (NX - 1), NZ, 16, 256), BF16),
        ((2, NZ, 16, 256), F32), ((2, NZ, 16, 256), BF16), ((2 * (NZ - 1), 16, 256), BF16),
    ]
    results = pl.pallas_call(
        kernel,
        out_shape=(
            pltpu.VMEM((128, 4608), BF16),
            pltpu.VMEM((32, 576), F32),
            pltpu.VMEM((8, 1024), F32),
        ),
        in_specs=[anywhere] * 6 + [vmem],
        out_specs=(vmem, vmem, vmem),
        scratch_shapes=[pltpu.VMEM(shape, kind) for shape, kind in shapes]
        + [
            dma((6,)), dma, dma((2,)), dma((2,)), dma, dma,
            dma((NY - 1,)), dma((NY - 1,)), dma((NY - 1,)), dma((NY - 1,)), dma, dma,
            dma((2 * NX,)), dma((2 * NX,)), dma((2 * NX - 2,)), dma((2 * NX - 2,)),
            dma((2 * NZ - 2,)), dma((2 * NZ - 2,)),
            pltpu.SemaphoreType.REGULAR((3,)),
        ],
        compiler_params=pltpu.CompilerParams(
            collective_id=0, has_side_effects=True, vmem_limit_bytes=58 << 20
        ),
        name="latent_attention_backward",
    )(queries, latents.T, up_value, grad_out, out_saved, log_sums.T, doc_starts)
    return pl.pallas_call(
        settle_kernel,
        out_shape=tuple(jax.ShapeDtypeStruct(r.shape, r.dtype) for r in results),
        in_specs=[vmem] * 3,
        out_specs=(anywhere,) * 3,
        scratch_shapes=[dma((3,))],
        name="settle",
    )(*[pltpu.with_memory_space_constraint(r, pltpu.VMEM) for r in results])


def solution(mesh):
    return jax.shard_map(
        on_device,
        mesh=mesh,
        in_specs=(
            P("ctx", "head"),
            P("ctx", None),
            P(None, "head"),
            P("ctx", "head"),
            P("ctx", "head"),
            P("ctx", "head"),
            P(),
        ),
        out_specs=(P("ctx", "head"), P(("ctx", "head"), None), P("ctx", "head")),
        check_vma=False,
    )
```

```python
import jax
import jax.numpy as jnp
from jax import lax
from jax.experimental import pallas as pl
from jax.experimental.pallas import tpu as pltpu
from jax.sharding import PartitionSpec as P

SCALE = 192.0 ** (-0.5)
MESH = pl.DeviceIdType.MESH
NX, NZ, NC, NY = 4, 8, 2, 8
CTX = NX * NZ * NC
F32, BF16 = jnp.float32, jnp.bfloat16
OWN, NEAR, FAR = (0, 256), (256, 256), (512, 128)


def dot(a, b, ca, cb):
    return lax.dot_general(a, b, (((ca,), (cb,)), ((), ())), preferred_element_type=F32)


def kernel(
    q_hbm, ct_hbm, w_hbm, g_hbm, o_hbm, ls_hbm, ds_ref,
    gq_hbm, gl_ref, gw_ref,
    qv, wv, gv, ov, lsv, win, qs, gl, pb, gs, ol, gqv, delta, lsc,
    gko, nbuf, nrecv, ya, yarecv, yb, ybrecv, ybsum, bsend, brecv,
    tv, crecv, xsend, xrecv, zpart, zsend, zrecv,
    s_in, s_out, s_sh, r_sh, s_n, r_n, s_ya, r_ya, s_yb, r_yb, s_b, r_b,
    s_c, r_c, s_x, r_x, s_z, r_z, known,
):
    d, y = lax.axis_index("ctx"), lax.axis_index("head")
    z, x, c = d // 8, lax.rem(d // 2, 4), lax.rem(d, 2)
    ring = lambda step: (lax.rem(d + step + CTX, CTX), y)
    partner = (d + 1 - 2 * c, y)
    at_x = lambda step: (z * 8 + lax.rem(x + step, 4) * 2 + c, y)
    at_z = lambda step: (lax.rem(z + step, 8) * 8 + x * 2 + c, y)
    at_y = lambda step: (d, lax.rem(y + step, 8))

    def remote(src, dst, send, recv, to):
        return pltpu.make_async_remote_copy(src, dst, send, recv, to, MESH)

    feats = pl.ds(64, 576)
    loads = [
        pltpu.make_async_copy(ct_hbm, win.at[feats, pl.ds(0, 256)], s_in.at[0]),
        pltpu.make_async_copy(g_hbm, gv, s_in.at[1]),
        pltpu.make_async_copy(w_hbm, wv, s_in.at[2]),
        pltpu.make_async_copy(q_hbm, qv, s_in.at[3]),
        pltpu.make_async_copy(ls_hbm, lsv, s_in.at[4]),
        pltpu.make_async_copy(o_hbm, ov, s_in.at[5]),
    ]
    for load in loads:
        load.start()

    sides = [at_y(1), at_y(NY - 1), at_z(1), at_z(NZ - 1)]

    def tell(level):
        for side in sides:
            pl.semaphore_signal(known.at[level], inc=1, device_id=side, device_id_type=MESH)

    def hear(level):
        pl.semaphore_wait(known.at[level], len(sides))

    peers = (
        [ring(1), ring(-1), ring(2), ring(-2), partner]
        + [at_x(k) for k in range(1, NX)]
        + sides
    )
    entry = pltpu.get_barrier_semaphore()
    for peer in peers:
        pl.semaphore_signal(entry, inc=1, device_id=peer, device_id_type=MESH)
    win[pl.ds(0, 64), :] = jnp.zeros((64, 640), BF16)
    win[pl.ds(640, 64), :] = jnp.zeros((64, 640), BF16)
    loads[0].wait()
    pl.semaphore_wait(entry, len(peers))
    near = remote(
        win.at[feats, pl.ds(0, 256)], win.at[feats, pl.ds(256, 256)], s_sh.at[0], r_sh.at[0],
        ring(1),
    )
    far = remote(
        win.at[feats, pl.ds(128, 128)], win.at[feats, pl.ds(512, 128)], s_sh.at[1], r_sh.at[1],
        ring(2),
    )
    near.start()
    far.start()
    tell(0)

    for load in loads[1:3]:
        load.wait()
    for par in range(2):
        for i in range(4):
            rows = pl.ds(i * 128, 128)
            cols = pl.ds((2 * i + par) * 128, 128)
            gl[par, rows, :] = dot(gv[:, cols], wv[:, cols], 1, 1).astype(BF16)
    for load in loads[3:]:
        load.wait()
    lsc[...] = lsv[...].T
    for par in range(2):
        for i in range(4):
            rows = pl.ds(i * 128, 128)
            h = 2 * i + par
            cols = pl.ds(h * 128, 128)
            qs[par, rows, :] = qv[:, pl.ds(i * 1152 + par * 512, 640)]
            delta[:, pl.ds(h, 1)] = jnp.sum(
                gv[:, cols].astype(F32) * ov[:, cols].astype(F32), axis=1, keepdims=True
            )
    qpos = d * 256 + 128 + lax.broadcasted_iota(jnp.int32, (128, 1), 0)
    starts = ds_ref[...].reshape(1, 257)
    begin = jnp.max(jnp.where(starts <= qpos, starts, 0), axis=1, keepdims=True)

    def attend(par, block, base):
        first, count = block
        lanes = pl.ds(first, count)
        score = dot(qs[par], win[pl.ds(64 - 64 * par, 640), lanes], 1, 0)
        gprob = dot(gl[par], win[pl.ds(64, 512), lanes], 1, 0)
        kpos = base + lax.broadcasted_iota(jnp.int32, (128, count), 1)
        allowed = (kpos >= begin) & (kpos <= qpos)
        for i in range(4):
            rows = pl.ds(i * 128, 128)
            part = slice(i * 128, (i + 1) * 128)
            h = pl.ds(2 * i + par, 1)
            prob = jnp.where(allowed, jnp.exp(score[part] * SCALE - lsc[:, h]), 0.0)
            pb[par, rows, lanes] = prob.astype(BF16)
            gs[par, rows, lanes] = (prob * (gprob[part] - delta[:, h]) * SCALE).astype(BF16)
        part = dot(pb[par, :, lanes], win[pl.ds(64, 512), lanes], 1, 1)
        return part

    def key_grad(block):
        lanes = pl.ds(*block)
        even = dot(gs[0, :, lanes], qs[0], 0, 0)
        odd = pltpu.roll(dot(gs[1, :, lanes], qs[1], 0, 0), 576, 1)
        value = dot(pb[0, :, lanes], gl[0], 0, 0) + dot(pb[1, :, lanes], gl[1], 0, 0)
        both = even + odd
        return jnp.concatenate([both[:, :512] + value, both[:, 512:576]], axis=1)

    ol[0] = attend(0, OWN, d * 256)
    hear(0)
    tell(1)
    ol[1] = attend(1, OWN, d * 256)
    hear(1)
    tell(2)
    gko[...] = key_grad(OWN)
    hear(2)

    whole = remote(nbuf, nrecv, s_n, r_n, partner)
    half = remote(nbuf.at[pl.ds(128, 128)], nrecv.at[pl.ds(0, 128)], s_n, r_n, partner)
    yas = [
        remote(
            ya.at[lax.rem(y + k, 8)], yarecv.at[k - 1], s_ya.at[k - 1], r_ya.at[k - 1], at_y(k)
        )
        for k in range(1, NY)
    ]
    ybs = [
        remote(
            yb.at[lax.rem(y + k, 8)], ybrecv.at[k - 1], s_yb.at[k - 1], r_yb.at[k - 1], at_y(k)
        )
        for k in range(1, NY)
    ]

    def send_own():
        ya[...] = gko[...].reshape(NY, 32, 576).astype(BF16)
        for copy in yas:
            copy.start()

    def attend_near(par):
        ol[par] += attend(par, NEAR, d * 256 - 256)

    @pl.when(c == 1)
    def _():
        send_own()
        near.wait_recv()
        attend_near(0)
        attend_near(1)
        nbuf[...] = key_grad(NEAR).astype(BF16)
        whole.start()

    @pl.when(c == 0)
    def _():
        near.wait_recv()
        attend_near(0)

    far.wait_recv()

    cores, xs, zs = [[], []], [[], []], [[], []]

    def up_grad(par):
        lat = (ol[par] + attend(par, FAR, d * 256 - 384)).astype(BF16)
        for i in range(2):
            low, high = [
                dot(
                    lat[j * 128 : (j + 1) * 128], gv[:, pl.ds((2 * j + par) * 128, 128)], 0, 0
                ).reshape(NZ * NX * NC, 8, 128)
                for j in (i, i + 2)
            ]
            term = jnp.concatenate([low, high], axis=1).astype(BF16)
            term = term.reshape(NZ, NX, NC, 16, 128)
            for xi in range(NX):
                for ci in range(NC):
                    tv[par, ci, xi, :, :, pl.ds(i * 128, 128)] = term[:, xi, ci]
        for k in range(1, NX + 1):
            xi = lax.rem(x + k, 4)
            j = par * NX + k - 1
            copy = remote(
                tv.at[par, 1 - c, xi], crecv.at[par, xi], s_c.at[j], r_c.at[j], partner
            )
            copy.start()
            cores[par].append(copy)

    def stage_x(par):
        for k in range(1, NX):
            xi = lax.rem(x + k, 4)
            j = par * (NX - 1) + k - 1
            cores[par][k - 1].wait_recv()
            xsend[j] = (tv[par, c, xi].astype(F32) + crecv[par, xi].astype(F32)).astype(BF16)
            copy = remote(xsend.at[j], xrecv.at[j], s_x.at[j], r_x.at[j], at_x(k))
            copy.start()
            xs[par].append(copy)
        cores[par][NX - 1].wait_recv()
        zpart[par] = tv[par, c, x].astype(F32) + crecv[par, x].astype(F32)

    def stage_z(par):
        part = zpart[par]
        for k in range(1, NX):
            xs[par][k - 1].wait_recv()
            part = part + xrecv[par * (NX - 1) + k - 1].astype(F32)
        zsend[par] = part.astype(BF16)
        for k in range(1, NZ):
            j = par * (NZ - 1) + k - 1
            copy = remote(
                zsend.at[par, lax.rem(z + k, 8)], zrecv.at[j], s_z.at[j], r_z.at[j], at_z(k)
            )
            copy.start()
            zs[par].append(copy)

    def finish(par):
        last = zsend[par, z].astype(F32)
        for k in range(1, NZ):
            zs[par][k - 1].wait_recv()
            last = last + zrecv[par * (NZ - 1) + k - 1].astype(F32)
        for side in range(2):
            for i in range(2):
                gw_ref[:, pl.ds((2 * i + par + 4 * side) * 128, 128)] = last[
                    side * 8 : side * 8 + 8, i * 128 : i * 128 + 128
                ]

    up_grad(0)

    @pl.when(c == 0)
    def _():
        attend_near(1)
        whole.wait_recv()
        gko[...] += nrecv[...].astype(F32)
        send_own()

    stage_x(0)
    up_grad(1)

    @pl.when(c == 0)
    def _():
        near_grad = key_grad(NEAR)
        nbuf[...] = near_grad.astype(BF16)
        half.start()
        yb[pl.ds(0, 4)] = near_grad[:128].reshape(4, 32, 576).astype(BF16)
        for k in range(1, NY):
            @pl.when(lax.rem(y + k, 8) < 4)
            def _():
                ybs[k - 1].start()

    def send_far():
        for k in range(1, NY):
            @pl.when(lax.rem(y + k, 8) >= 4)
            def _():
                ybs[k - 1].start()

    gkf = key_grad(FAR)

    @pl.when(c == 0)
    def _():
        yb[pl.ds(4, 4)] = gkf.reshape(4, 32, 576).astype(BF16)
        send_far()

    stage_x(1)

    @pl.when(c == 1)
    def _():
        half.wait_recv()
        yb[pl.ds(4, 4)] = (
            (gkf + nrecv[pl.ds(0, 128)].astype(F32)).reshape(4, 32, 576).astype(BF16)
        )
        send_far()

    def query_grad(par):
        return dot(gs[par], win[pl.ds(64 - 64 * par, 640), :], 1, 1)

    even = query_grad(0)
    stage_z(0)
    odd = query_grad(1)
    for i in range(4):
        rows = slice(i * 128, (i + 1) * 128)
        gq_hbm[:, pl.ds(i * 1152, 512)] = even[rows, :512].astype(BF16)
        gq_hbm[:, pl.ds(i * 1152 + 512, 128)] = (even[rows, 512:] + odd[rows, :128]).astype(BF16)
        gq_hbm[:, pl.ds(i * 1152 + 640, 512)] = odd[rows, 128:].astype(BF16)
    stage_z(1)

    back = remote(
        bsend, brecv, s_b, r_b, ring(jnp.where((c == 1) | (y >= 4), -2, -1))
    )

    @pl.when((c == 0) | (y >= 4))
    def _():
        mine = yb[y].astype(F32)
        for k in range(1, NY):
            ybs[k - 1].wait_recv()
            mine = mine + ybrecv[k - 1].astype(F32)
        bsend[...] = mine.astype(BF16)
        back.start()

    finish(0)
    mine = ya[y].astype(F32)
    for k in range(1, NY):
        yas[k - 1].wait_recv()
        mine = mine + yarecv[k - 1].astype(F32)
    gl_ref[...] = mine

    @pl.when((c == 1) | (y >= 4))
    def _():
        back.wait_recv()
        gl_ref[...] += brecv[...].astype(F32)

    finish(1)
    near.wait_send()
    far.wait_send()

    @pl.when(c == 1)
    def _():
        whole.wait_send()

    @pl.when(c == 0)
    def _():
        half.wait_send()

    for k in range(1, NY):
        @pl.when((c == 0) | (lax.rem(y + k, 8) >= 4))
        def _():
            ybs[k - 1].wait_send()

    @pl.when((c == 0) | (y >= 4))
    def _():
        back.wait_send()

    for copy in yas + cores[0] + cores[1] + xs[0] + xs[1] + zs[0] + zs[1]:
        copy.wait_send()


def settle_kernel(gq_in, gl_in, gw_in, gq_out, gl_out, gw_out, sem):
    pairs = [(gq_in, gq_out), (gl_in, gl_out), (gw_in, gw_out)]
    writes = [pltpu.make_async_copy(a, b, sem.at[i]) for i, (a, b) in enumerate(pairs)]
    for write in writes:
        write.start()
    for write in writes:
        write.wait()


def on_device(queries, latents, up_value, grad_out, out_saved, log_sums, doc_starts):
    anywhere = pl.BlockSpec(memory_space=pl.ANY)
    vmem = pl.BlockSpec(memory_space=pltpu.VMEM)
    dma = pltpu.SemaphoreType.DMA
    shapes = [
        ((128, 4608), BF16), ((512, 1024), BF16), ((128, 1024), BF16), ((128, 1024), BF16),
        ((8, 128), F32), ((704, 640), BF16), ((2, 512, 640), BF16), ((2, 512, 512), BF16),
        ((2, 512, 640), BF16), ((2, 512, 640), BF16), ((2, 512, 512), F32), ((128, 4608), BF16),
        ((128, 8), F32), ((128, 8), F32),
        ((256, 576), F32), ((256, 576), BF16), ((256, 576), BF16),
        ((NY, 32, 576), BF16), ((NY - 1, 32, 576), BF16),
        ((NY, 32, 576), BF16), ((NY - 1, 32, 576), BF16),
        ((32, 576), F32), ((32, 576), BF16), ((32, 576), BF16),
        ((2, 2, NX, NZ, 16, 256), BF16), ((2, NX, NZ, 16, 256), BF16),
        ((2 * (NX - 1), NZ, 16, 256), BF16), ((2 * (NX - 1), NZ, 16, 256), BF16),
        ((2, NZ, 16, 256), F32), ((2, NZ, 16, 256), BF16), ((2 * (NZ - 1), 16, 256), BF16),
    ]
    results = pl.pallas_call(
        kernel,
        out_shape=(
            pltpu.VMEM((128, 4608), BF16),
            pltpu.VMEM((32, 576), F32),
            pltpu.VMEM((8, 1024), F32),
        ),
        in_specs=[anywhere] * 6 + [vmem],
        out_specs=(vmem, vmem, vmem),
        scratch_shapes=[pltpu.VMEM(shape, kind) for shape, kind in shapes]
        + [
            dma((6,)), dma, dma((2,)), dma((2,)), dma, dma,
            dma((NY - 1,)), dma((NY - 1,)), dma((NY - 1,)), dma((NY - 1,)), dma, dma,
            dma((2 * NX,)), dma((2 * NX,)), dma((2 * NX - 2,)), dma((2 * NX - 2,)),
            dma((2 * NZ - 2,)), dma((2 * NZ - 2,)),
            pltpu.SemaphoreType.REGULAR((3,)),
        ],
        compiler_params=pltpu.CompilerParams(
            collective_id=0, has_side_effects=True, vmem_limit_bytes=58 << 20
        ),
        name="latent_attention_backward",
    )(queries, latents.T, up_value, grad_out, out_saved, log_sums.T, doc_starts)
    return pl.pallas_call(
        settle_kernel,
        out_shape=tuple(jax.ShapeDtypeStruct(r.shape, r.dtype) for r in results),
        in_specs=[vmem] * 3,
        out_specs=(anywhere,) * 3,
        scratch_shapes=[dma((3,))],
        name="settle",
    )(*[pltpu.with_memory_space_constraint(r, pltpu.VMEM) for r in results])


def solution(mesh):
    return jax.shard_map(
        on_device,
        mesh=mesh,
        in_specs=(
            P("ctx", "head"),
            P("ctx", None),
            P(None, "head"),
            P("ctx", "head"),
            P("ctx", "head"),
            P("ctx", "head"),
            P(),
        ),
        out_specs=(P("ctx", "head"), P(("ctx", "head"), None), P("ctx", "head")),
        check_vma=False,
    )
```
